512 devices in a mesh: seq: 32 (over y_hi, z, core), chan: 16 (over x, y_lo).
Axes of the slice: x: 4, y: 8 (y_hi: 2, y_lo: 4; y = y_hi * 4 + y_lo), z: 8, core: 2. Of those that a mesh axis runs over, the one named last changes fastest.
Arguments:
- values: bfloat16 [4096, 1024], P('seq', 'chan'), may hold values from -6 to 6
- gate_inner: bfloat16 [4096, 1024], P('seq', 'chan'), may hold values from -6 to 6
- gate_outer: bfloat16 [4096, 1024], P('seq', 'chan'), may hold values from -6 to 6
- filter_one: float32 [16, 4096], P('chan', 'seq'), may hold values from -0.09375 to 0.09375
- filter_two: float32 [16, 4096], P('chan', 'seq'), may hold values from -0.09375 to 0.09375
- teacher: bfloat16 [4096, 1024], P('seq', 'chan'), may hold values from -6 to 6
- w_out: bfloat16 [1024, 1024], P(None, 'chan'), may hold values from -0.1875 to 0.1875
- gene_ids: int32 [4096], P('seq'), may hold values from 0 to 25425
- cell_lengths: int32 [4], replicated, may hold values from 1 to 2048, 4096 in all
- gene_weights: float32 [25426], replicated, may hold values from 0.5 to 2
Outputs:
- grad_values: bfloat16 [4096, 1024], P('seq', 'chan')
- grad_inner: bfloat16 [4096, 1024], P('seq', 'chan')
- grad_outer: bfloat16 [4096, 1024], P('seq', 'chan')
- grad_filter_one: float32 [16, 4096], P('chan', 'seq')
- grad_filter_two: float32 [16, 4096], P('chan', 'seq')
- grad_w_out: float32 [1024, 1024], P('seq', 'chan')
The draws below stay inside these ranges and needn't reach their ends.
Inputs may be any that keep to these rules, and one draw needn't show every extreme that they name: `cell_lengths`: the lengths sum to 4096, and the largest equals 2048.
All inputs are finite; a program needn't handle non-finite values.
Results may differ from the reference program's by a relative error of at most 0.0051.
Values may be sent and summed in bfloat16 or wider, within the bound.
A program may use at most 64 MiB of HBM per device.

```python
import math
import jax
import jax.numpy as jnp
import numpy as np

D = 1024
GROUPS = 16
VOCAB = 25426
CELL_MOST = 2048
SEQ = 4096
CELLS = 4


def place_ends(values, own_key, smallest, high):
    longest = values.shape.index(max(values.shape))
    spots = []
    for shift in (0, 1):
        where = [jax.random.randint(jax.random.fold_in(own_key, axis), (), 0, length) for axis, length in enumerate(values.shape)]
        where[longest] = (where[longest] + shift) % values.shape[longest]
        spots.append(tuple(where))
    return values.at[spots[0]].set(smallest).at[spots[1]].set(high)


def levels(rng, extent, shards, least, top_value):
    def one(dim, parts):
        draws = jax.random.uniform(jax.random.fold_in(jax.random.fold_in(rng, 6), dim), (parts,), jnp.float32, least / len(shards), top_value / len(shards))
        return jnp.repeat(jnp.exp(draws), extent[dim] // parts).reshape((-1,) + (1,) * (len(extent) - dim - 1))

    loudness = one(*shards[0])
    for cut in shards[1:]:
        loudness = loudness * one(*cut)
    return loudness


def rank_table(count, slope):
    weights = [(1 << 20) // math.isqrt(grade ** slope) + 1 for grade in range(1, count + 1)]
    width = 1 + sum(weights) // (1 << 30)
    return np.cumsum(np.array([max(1, weight // width) for weight in weights]))


def ranked(key, extent, amount, skew):
    grid = rank_table(amount, skew)
    pick = jax.random.randint(jax.random.fold_in(key, 1), extent, 0, int(grid[amount - 1]))
    rank = jnp.searchsorted(jnp.asarray(grid, jnp.int32), pick, side="right")
    return jax.random.permutation(jax.random.fold_in(key, 2), amount)[rank].astype(jnp.int32)


def length_profile(count, total, limit, slope):
    loads = [(1 << 20) // math.isqrt(standing ** slope) + 1 for standing in range(2, count + 1)]
    spare, holding = total - limit - (count - 1), [1] * (count - 1)
    while spare > 0:
        candidates = [i for i in range(count - 1) if holding[i] < limit]
        mass, budget = sum([loads[i] for i in candidates]), spare
        for i in candidates:
            extra = min(limit - holding[i], max(1, budget * loads[i] // mass), spare)
            holding[i] = holding[i] + extra
            spare = spare - extra
    return np.array([limit] + holding)


def uneven_parts(rng, count, total, bound, skew):
    if count == 2:
        one = jax.random.randint(rng, (), max(1, total - bound), min(bound, total - 1) + 1)
        return jnp.stack([one, total - one])
    sizes = jnp.asarray(length_profile(count, total, bound, skew), jnp.int32)
    twos = (count - 1) // 2
    donor, receiver = sizes[1:1 + 2 * twos:2], sizes[2:2 + 2 * twos:2]
    room = jnp.minimum(donor - 1, bound - receiver)
    moved = jax.random.randint(jax.random.fold_in(rng, 1), (twos,), 0, 1 << 20) % (room + 1)
    sizes = sizes.at[1:1 + 2 * twos:2].set(donor - moved).at[2:2 + 2 * twos:2].set(receiver + moved)
    return sizes[jax.random.permutation(jax.random.fold_in(rng, 2), count)]


def noise(key, dims, scale, most, pieces=(), kind=jnp.bfloat16):
    values = scale * jax.random.normal(key, dims, jnp.float32)
    if pieces:
        values = values * levels(key, dims, pieces, -0.22, 0.18)
    return jnp.clip(values, -most, most).astype(kind)


def setup_inputs(seed: int = 0) -> dict:
    key_of = jax.random.split(jax.random.key(seed), 11)
    return {
        "values": noise(key_of[0], (SEQ, D), 1.0, 6.0, ((0, 32), (1, 16))),
        "gate_inner": noise(key_of[1], (SEQ, D), 1.0, 6.0, ((0, 32), (1, 16))),
        "gate_outer": noise(key_of[2], (SEQ, D), 1.0, 6.0, ((0, 32), (1, 16))),
        "filter_one": noise(key_of[3], (GROUPS, SEQ), SEQ ** -0.5, 0.09375, ((0, 16), (1, 32)), jnp.float32),
        "filter_two": noise(key_of[4], (GROUPS, SEQ), SEQ ** -0.5, 0.09375, ((0, 16), (1, 32)), jnp.float32),
        "teacher": noise(key_of[5], (SEQ, D), 1.0, 6.0, ((0, 32), (1, 16))),
        "w_out": noise(key_of[6], (D, D), D ** -0.5, 0.1875, ((1, 16),)),
        "gene_ids": place_ends(ranked(key_of[7], (SEQ,), VOCAB, 2), jax.random.fold_in(key_of[7], 3), 0, VOCAB - 1).astype(jnp.int32),
        "cell_lengths": uneven_parts(key_of[8], CELLS, SEQ, CELL_MOST, 0).astype(jnp.int32),
        "gene_weights": jnp.clip(jnp.exp(jax.random.uniform(key_of[9], (VOCAB,), jnp.float32, math.log(0.5), math.log(2.0))), 0.5, 2.0),
    }


def reference(values, gate_inner, gate_outer, filter_one, filter_two, teacher, w_out, gene_ids, cell_lengths, gene_weights):
    length = values.shape[0]
    padded = 2 * length
    group_width = D // GROUPS

    def forward(signal):
        return jnp.fft.rfft(signal, n=padded, axis=0)

    def inverse(spectra):
        return jnp.fft.irfft(spectra, n=padded, axis=0)[:length]

    def pool_groups(product):
        summed = product.reshape(product.shape[0], GROUPS, group_width).sum(axis=2)
        return inverse(summed).T

    spec_one = forward(filter_one.T)
    spec_two = forward(filter_two.T)
    wide_one = jnp.repeat(spec_one, group_width, axis=1)
    wide_two = jnp.repeat(spec_two, group_width, axis=1)
    spec_values = forward(values.astype(jnp.float32))
    first_conv = inverse(wide_one * spec_values)
    inner_f = gate_inner.astype(jnp.float32)
    outer_f = gate_outer.astype(jnp.float32)
    inner_prod = inner_f * first_conv
    spec_inner = forward(inner_prod)
    second_conv = inverse(wide_two * spec_inner)
    pooled_out = (outer_f * second_conv).astype(jnp.bfloat16)
    output = jnp.dot(pooled_out, w_out, preferred_element_type=jnp.float32)
    position = jnp.arange(length, dtype=jnp.int32)
    starts = (jnp.cumsum(cell_lengths) - cell_lengths).astype(jnp.int32)
    opening = jnp.any(position[:, None] == starts[None, :], axis=1)
    weights = gene_weights[gene_ids] * jnp.where(opening, 0.0, 1.0).astype(jnp.float32)
    deviation = (weights[:, None] * (output - teacher.astype(jnp.float32))).astype(jnp.bfloat16)
    grad_w_out = jnp.dot(pooled_out.T, deviation, preferred_element_type=jnp.float32)
    back_outer = jnp.dot(deviation, w_out.T, preferred_element_type=jnp.float32)
    grad_outer = (back_outer * second_conv).astype(jnp.bfloat16)
    back_second = back_outer * outer_f
    spec_second = forward(back_second)
    back_inner = inverse(jnp.conj(wide_two) * spec_second)
    grad_filter_two = pool_groups(jnp.conj(spec_inner) * spec_second)
    grad_inner = (back_inner * first_conv).astype(jnp.bfloat16)
    back_first = back_inner * inner_f
    spec_first = forward(back_first)
    grad_values = inverse(jnp.conj(wide_one) * spec_first).astype(jnp.bfloat16)
    grad_filter_one = pool_groups(jnp.conj(spec_values) * spec_first)
    return (grad_values, grad_inner, grad_outer, grad_filter_one, grad_filter_two, grad_w_out)
```

```python
import functools

import jax
import jax.numpy as jnp
from jax import lax
from jax.experimental import pallas as pl
from jax.experimental.pallas import tpu as pltpu
from jax.sharding import PartitionSpec as P

F32 = jnp.float32
BF16 = jnp.bfloat16
MESH = pl.DeviceIdType.MESH
HIGHEST = lax.Precision.HIGHEST
LANES = 128


def nn(left, right, precision=None):
    return lax.dot_general(
        left, right, (((1,), (0,)), ((), ())), precision=precision, preferred_element_type=F32
    )


def nt(left, right):
    return lax.dot_general(left, right, (((1,), (1,)), ((), ())), preferred_element_type=F32)


def tn(left, right, precision=None):
    return lax.dot_general(
        left, right, (((0,), (0,)), ((), ())), precision=precision, preferred_element_type=F32
    )


def split(value):
    high = value.astype(BF16)
    return high, (value - high.astype(F32)).astype(BF16)


def multiple(index, factor):
    return pl.multiple_of(index * factor, factor)


def kernel(
    blocks,
    groups,
    values,
    gate_inner,
    gate_outer,
    teacher,
    filter_one,
    filter_two,
    w_out,
    gene_ids,
    cell_lengths,
    table,
    out_values,
    out_inner,
    out_outer,
    out_one,
    out_two,
    out_w,
    stage,
    send1,
    recv1,
    flat1,
    pad_one,
    pad_two,
    gate_c,
    conv_c,
    lags_one,
    lags_two,
    big_one,
    big_two,
    toe_one,
    toe_two,
    strip_one,
    strip_two,
    send2,
    recv2,
    second_t,
    outer_t,
    teach_t,
    w_blocks,
    w_rows,
    token_w,
    pooled_t,
    pooled_all,
    dev_t,
    dev_all,
    gw_send,
    gw_recv,
    send5,
    recv5,
    flat5,
    big_back,
    cross,
    sums,
    flat6,
    send6,
    recv6,
    send_sem,
    recv_sem,
):
    half_count = blocks // 2
    channels = values.shape[0]
    share = channels // half_count
    rows = share * blocks
    own_rows = share * half_count
    row1 = send1.shape[1]
    row6 = send6.shape[1]
    s = lax.axis_index("seq")
    g = lax.axis_index("chan")
    half = lax.div(s, half_count)
    place = lax.rem(s, half_count)

    barrier = pltpu.get_barrier_semaphore()

    def greet_seq(step, carry):
        pl.semaphore_signal(
            barrier, inc=1, device_id={"seq": lax.rem(s + step, blocks)}, device_id_type=MESH
        )
        return carry

    def greet_chan(step, carry):
        pl.semaphore_signal(
            barrier, inc=1, device_id={"chan": lax.rem(g + step, groups)}, device_id_type=MESH
        )
        return carry

    lax.fori_loop(1, blocks, greet_seq, 0)
    lax.fori_loop(1, groups, greet_chan, 0)

    def remote(src, dst, index, device):
        return pltpu.make_async_remote_copy(
            src_ref=src,
            dst_ref=dst,
            send_sem=send_sem.at[index],
            recv_sem=recv_sem.at[index],
            device_id=device,
            device_id_type=MESH,
        )

    def to_seq(index, src_of, dst):
        def body(step, carry):
            peer = lax.rem(s + step, blocks)
            remote(src_of(peer), dst, index, {"seq": peer}).start()
            return carry

        lax.fori_loop(1, blocks, body, 0)
        pltpu.make_async_copy(src_of(s), dst, recv_sem.at[index]).start()

    def to_half(index, src_of, dst):
        def body(step, carry):
            peer = lax.rem(place + step, half_count)
            remote(src_of(peer), dst, index, {"seq": half * half_count + peer}).start()
            return carry

        lax.fori_loop(1, half_count, body, 0)
        pltpu.make_async_copy(src_of(place), dst, recv_sem.at[index]).start()

    def to_chan(index, src_of, dst):
        def body(step, carry):
            peer = lax.rem(g + step, groups)
            remote(src_of(peer), dst, index, {"chan": peer}).start()
            return carry

        lax.fori_loop(1, groups, body, 0)
        pltpu.make_async_copy(src_of(g), dst, recv_sem.at[index]).start()

    def arrived(index, ref):
        pltpu.make_async_copy(ref, ref, recv_sem.at[index]).wait()

    def sent(index, ref):
        pltpu.make_async_copy(ref, ref, send_sem.at[index]).wait()

    values_t = values[...].astype(F32)
    inner_t = gate_inner[...].astype(F32)
    high_one, low_one = split(filter_one[...])
    high_two, low_two = split(filter_two[...])
    filter_rows = jnp.concatenate(
        [high_one.astype(F32), low_one.astype(F32), high_two.astype(F32), low_two.astype(F32)], axis=0
    )
    for p in range(half_count):
        stage[p, 0:share, :] = values_t[p * share : (p + 1) * share]
        stage[p, share : 2 * share, :] = inner_t[p * share : (p + 1) * share]
        stage[p, 2 * share : 2 * share + 4, :] = filter_rows
        if 2 * share + 4 < row1:
            stage[p, 2 * share + 4 : row1, :] = jnp.zeros((row1 - 2 * share - 4, LANES), F32)
    send1[...] = stage[...].astype(BF16)
    pl.semaphore_wait(barrier, blocks + groups - 2)
    to_seq(0, lambda peer: send1.at[lax.rem(peer, half_count)], recv1.at[s])
    to_chan(
        1,
        lambda peer: w_out.at[:, pl.ds(multiple(lax.div(peer, 2), LANES), LANES)],
        w_blocks.at[g],
    )

    outer_t[...] = gate_outer[...].astype(F32)
    teach_t[...] = teacher[...].astype(F32)
    ids = gene_ids[...]
    hot_rows = (
        lax.broadcasted_iota(jnp.int32, (table.shape[0], LANES), 0) == lax.shift_right_logical(ids, 7)
    ).astype(F32)
    picked = tn(table[...], hot_rows, HIGHEST)
    hot_lanes = lax.broadcasted_iota(jnp.int32, (LANES, LANES), 0) == jnp.bitwise_and(ids, 127)
    weight = jnp.sum(jnp.where(hot_lanes, picked, 0.0), axis=0, keepdims=True)
    token = s * LANES + lax.broadcasted_iota(jnp.int32, (1, LANES), 1)
    opening = token == 0
    start = cell_lengths[0]
    for cell in range(1, cell_lengths.shape[0]):
        opening = jnp.logical_or(opening, token == start)
        start = start + cell_lengths[cell]
    token_w[...] = jnp.where(opening, 0.0, weight)

    row_iota = lax.broadcasted_iota(jnp.int32, (LANES, LANES), 0)
    lane_iota = lax.broadcasted_iota(jnp.int32, (LANES, LANES), 1)
    keep = lane_iota >= row_iota
    flip = (row_iota + lane_iota == LANES - 1).astype(BF16)

    arrived(0, recv1)
    flat1[...] = recv1[...].astype(F32).reshape(blocks * row1, LANES)

    def every(ref, first, stride):
        return ref[pl.ds(first, blocks, stride=stride), :]

    zeros = jnp.zeros((blocks, LANES), F32)
    for c in range(share):
        pad_one[c, 0:blocks, :] = zeros
        pad_one[c, blocks : 2 * blocks, :] = every(flat1, c, row1)
        pad_two[c, 0:blocks, :] = zeros
        gate_c[c * blocks : (c + 1) * blocks, :] = every(flat1, share + c, row1)
    lags_one[...] = every(flat1, 2 * share, row1) + every(flat1, 2 * share + 1, row1)
    lags_two[...] = every(flat1, 2 * share + 2, row1) + every(flat1, 2 * share + 3, row1)

    def toeplitz(lags, toe):
        def body(m, before):
            row = lags[pl.ds(m, 1), :]
            turned = pltpu.roll(
                jnp.broadcast_to(row, (LANES, LANES)), 0, axis=1, stride=1, stride_axis=0
            )
            high, low = split(jnp.where(keep, turned, before))
            at = pl.ds(multiple(m, LANES), LANES)
            toe[at, 0:LANES] = high
            toe[at, LANES : 2 * LANES] = low
            return turned

        lax.fori_loop(0, blocks, body, jnp.zeros((LANES, LANES), F32))

    def stripe(toe, strip):
        def body(m, carry):
            at = pl.ds(multiple(m, LANES), LANES)
            strip[0:LANES, at] = toe[at, 0:LANES]
            strip[LANES : 2 * LANES, at] = toe[at, LANES : 2 * LANES]
            return carry

        lax.fori_loop(0, blocks, body, 0)

    def spread(pad, big, backward):
        for m in range(blocks):
            first = m if backward else blocks - m
            for c in range(share):
                big[c * blocks : (c + 1) * blocks, m * LANES : (m + 1) * LANES] = pad[
                    c, first : first + blocks, :
                ].astype(BF16)

    length = blocks * LANES

    def own(read):
        return jnp.concatenate(
            [
                read(pl.ds(pl.multiple_of(c * blocks + half * half_count, half_count), half_count))
                for c in range(share)
            ],
            axis=0,
        )

    def joined(product):
        return product[:, 0:LANES] + product[:, LANES : 2 * LANES]

    spread(pad_one, big_one, False)
    toeplitz(lags_one, toe_one)
    first_conv = joined(nn(big_one[:, 0:length], toe_one[...]))
    conv_c[...] = first_conv
    inner_prod = gate_c[...] * first_conv
    for c in range(share):
        pad_two[c, blocks : 2 * blocks, :] = inner_prod[c * blocks : (c + 1) * blocks]
    spread(pad_two, big_two, False)
    toeplitz(lags_two, toe_two)
    second = joined(nn(own(lambda at: big_two[at, 0:length]), toe_two[...]))
    row2 = send2.shape[0] // half_count
    for c in range(share):
        send2[pl.ds(c, half_count, stride=row2), :] = second[c * half_count : (c + 1) * half_count]
    to_half(
        2,
        lambda peer: send2.at[pl.ds(multiple(peer, row2), row2), :],
        recv2.at[pl.ds(multiple(place, row2), row2), :],
    )
    stripe(toe_two, strip_two)
    stripe(toe_one, strip_one)
    arrived(1, w_blocks)
    stacked = w_blocks[...].astype(F32).reshape(groups * channels, LANES)
    w_rows[...] = stacked.T.astype(BF16)

    arrived(2, recv2)
    for p in range(half_count):
        second_t[p * share : (p + 1) * share, :] = recv2[p * row2 : p * row2 + share, :]
    pooled_t[...] = (outer_t[...] * second_t[...]).astype(BF16)
    to_chan(3, lambda peer: pooled_t, pooled_all.at[g])
    arrived(3, pooled_all)
    width = groups * channels
    pooled = pooled_all[...].reshape(width, LANES)
    output = nn(w_out[...], pooled)
    deviation = (token_w[...] * (output - teach_t[...])).astype(BF16)
    dev_t[...] = deviation
    to_chan(4, lambda peer: dev_t, dev_all.at[g])

    share_w = width // blocks
    part = share_w // 2
    parts = pooled.reshape(blocks, 2, part, LANES)
    left = jnp.concatenate(
        [parts[:, 0].reshape(blocks * part, LANES), parts[:, 1].reshape(blocks * part, LANES)], axis=1
    )
    empty = jnp.zeros_like(deviation)
    right = jnp.concatenate(
        [jnp.concatenate([deviation, empty], axis=1), jnp.concatenate([empty, deviation], axis=1)], axis=0
    )
    gw_send[...] = nt(left, right).reshape(blocks, part, LANES).astype(gw_send.dtype)
    to_seq(5, lambda peer: gw_send.at[peer], gw_recv.at[s])

    arrived(4, dev_all)
    back_outer = nn(w_rows[pl.ds(multiple(lax.rem(g, 2), channels), channels), :], dev_all[...].reshape(width, LANES))
    back_second = back_outer * outer_t[...]
    send5[...] = back_second.astype(BF16).reshape(half_count, share, LANES)
    to_seq(6, lambda peer: send5.at[lax.rem(peer, half_count)], recv5.at[s])
    out_outer[...] = (back_outer * second_t[...]).astype(BF16)

    arrived(6, recv5)
    flat5[...] = recv5[...].astype(F32).reshape(rows, LANES)
    signal = [every(flat5, c, share) for c in range(share)]
    for c in range(share):
        pad_two[c, 0:blocks, :] = signal[c]
        pad_two[c, blocks : 2 * blocks, :] = zeros
    spread(pad_two, big_back, True)
    back_inner = joined(nt(big_back[...], strip_two[...]))
    back_first = back_inner * gate_c[...]
    for c in range(share):
        pad_one[c, 0:blocks, :] = back_first[c * blocks : (c + 1) * blocks]
        pad_one[c, blocks : 2 * blocks, :] = zeros
    grad_inner_c = back_inner * conv_c[...]
    conv_c[...] = grad_inner_c

    def filter_grad(back, big, column):
        turned = nt(flip, back.astype(BF16)).astype(BF16)
        window = big[:, pl.ds(multiple(half, half_count * LANES), (half_count + 1) * LANES)]
        cross[...] = nn(turned, window)

        def rolled(m):
            at = pl.ds(multiple(m, LANES), LANES)
            return pltpu.roll(cross[:, at], 0, axis=1, stride=1, stride_axis=0)

        def body(m, current):
            later = rolled(m + 1)
            sums[pl.ds(m, 1), :] = jnp.sum(jnp.where(keep, current, later), axis=0, keepdims=True)
            return later

        lax.fori_loop(0, half_count, body, rolled(0))
        high, low = split(sums[...])
        flat6[pl.ds(column, half_count, stride=row6), :] = high.astype(F32)
        flat6[pl.ds(column + 1, half_count, stride=row6), :] = low.astype(F32)

    for big in (big_one, big_two):
        big[:, length : length + LANES] = jnp.zeros((rows, LANES), BF16)
    filter_grad(jnp.concatenate(signal, axis=0), big_two, 2 * share + 2)
    filter_grad(back_first, big_one, 2 * share)
    spread(pad_one, big_back, True)
    grad_values_c = joined(nt(own(lambda at: big_back[at, :]), strip_one[...]))
    grad_inner_own = own(lambda at: conv_c[at, :])
    for c in range(share):
        at = slice(c * half_count, (c + 1) * half_count)
        flat6[pl.ds(c, half_count, stride=row6), :] = grad_values_c[at]
        flat6[pl.ds(share + c, half_count, stride=row6), :] = grad_inner_own[at]
    for c in range(2 * share + 4, row6):
        flat6[pl.ds(c, half_count, stride=row6), :] = jnp.zeros((half_count, LANES), F32)
    send6[...] = flat6[...].reshape(half_count, row6, LANES).astype(BF16)
    to_half(7, lambda peer: send6.at[peer], recv6.at[place])

    arrived(5, gw_recv)
    total_w = jnp.sum(gw_recv[...].astype(F32), axis=0)
    out_w[0:part, :] = total_w[:, 0:channels]
    out_w[part:share_w, :] = total_w[:, channels : 2 * channels]

    arrived(7, recv6)
    flat6[...] = recv6[...].astype(F32).reshape(half_count * row6, LANES)
    for p in range(half_count):
        second_t[p * share : (p + 1) * share, :] = flat6[p * row6 : p * row6 + share, :]
        outer_t[p * share : (p + 1) * share, :] = flat6[p * row6 + share : p * row6 + 2 * share, :]
    out_values[...] = second_t[...].astype(BF16)
    out_inner[...] = outer_t[...].astype(BF16)
    lag_rows = []
    for column in (2 * share, 2 * share + 2):
        both = flat6[pl.ds(column, half_count, stride=row6), :] + flat6[
            pl.ds(column + 1, half_count, stride=row6), :
        ]
        lag_rows.append(jnp.sum(both, axis=0, keepdims=True))
    lag_rows.append(jnp.zeros((6, LANES), F32))
    ordered = nn(jnp.concatenate(lag_rows, axis=0), flip.astype(F32), HIGHEST)
    out_one[...] = ordered[0:1]
    out_two[...] = ordered[1:2]

    sent(0, recv1.at[pl.ds(0, blocks - 1)])
    sent(1, w_blocks.at[pl.ds(0, groups - 1)])
    sent(2, recv2.at[pl.ds(0, row2 * (half_count - 1)), :])
    sent(3, pooled_all.at[pl.ds(0, groups - 1)])
    sent(4, dev_all.at[pl.ds(0, groups - 1)])
    sent(5, gw_recv.at[pl.ds(0, blocks - 1)])
    sent(6, recv5.at[pl.ds(0, blocks - 1)])
    sent(7, recv6.at[pl.ds(0, half_count - 1)])


def rounded(count, factor):
    return -(-count // factor) * factor


def per_device(
    blocks,
    groups,
    values,
    gate_inner,
    gate_outer,
    filter_one,
    filter_two,
    teacher,
    w_out,
    gene_ids,
    cell_lengths,
    gene_weights,
):
    length, channels = values.shape
    half_count = blocks // 2
    share = channels // half_count
    rows = share * blocks
    width = groups * channels
    share_w = width // blocks
    row1 = rounded(2 * share + 4, 16)
    row2 = rounded(share, 8)
    span = blocks * LANES
    vocab = gene_weights.shape[0]
    padded = rounded(vocab, 8 * LANES)
    table = jnp.pad(gene_weights, (0, padded - vocab)).reshape(padded // LANES, LANES)
    vmem = pl.BlockSpec(memory_space=pltpu.VMEM)
    smem = pl.BlockSpec(memory_space=pltpu.SMEM)
    V = pltpu.VMEM
    grads = pl.pallas_call(
        functools.partial(kernel, blocks, groups),
        out_shape=(
            jax.ShapeDtypeStruct((channels, length), BF16),
            jax.ShapeDtypeStruct((channels, length), BF16),
            jax.ShapeDtypeStruct((channels, length), BF16),
            jax.ShapeDtypeStruct((1, LANES), F32),
            jax.ShapeDtypeStruct((1, LANES), F32),
            jax.ShapeDtypeStruct((share_w, channels), F32),
        ),
        in_specs=[vmem] * 8 + [smem, vmem],
        out_specs=(vmem,) * 6,
        scratch_shapes=[
            V((half_count, row1, LANES), F32),
            V((half_count, row1, LANES), BF16),
            V((blocks, row1, LANES), BF16),
            V((blocks * row1, LANES), F32),
            V((share, 2 * blocks, LANES), F32),
            V((share, 2 * blocks, LANES), F32),
            V((rows, LANES), F32),
            V((rows, LANES), F32),
            V((blocks, LANES), F32),
            V((blocks, LANES), F32),
            V((rows, span + LANES), BF16),
            V((rows, span + LANES), BF16),
            V((span, 2 * LANES), BF16),
            V((span, 2 * LANES), BF16),
            V((2 * LANES, span), BF16),
            V((2 * LANES, span), BF16),
            V((half_count * row2, LANES), F32),
            V((half_count * row2, LANES), F32),
            V((channels, LANES), F32),
            V((channels, LANES), F32),
            V((channels, LANES), F32),
            V((groups, channels, LANES), BF16),
            V((LANES, width), BF16),
            V((1, LANES), F32),
            V((channels, LANES), BF16),
            V((groups, channels, LANES), BF16),
            V((channels, LANES), BF16),
            V((groups, channels, LANES), BF16),
            V((blocks, share_w // 2, LANES), BF16),
            V((blocks, share_w // 2, LANES), BF16),
            V((half_count, share, LANES), BF16),
            V((blocks, share, LANES), BF16),
            V((rows, LANES), F32),
            V((rows, span), BF16),
            V((LANES, (half_count + 1) * LANES), F32),
            V((half_count, LANES), F32),
            V((half_count * row1, LANES), F32),
            V((half_count, row1, LANES), BF16),
            V((half_count, row1, LANES), BF16),
            pltpu.SemaphoreType.DMA((8,)),
            pltpu.SemaphoreType.DMA((8,)),
        ],
        compiler_params=pltpu.CompilerParams(
            collective_id=0, has_side_effects=True, vmem_limit_bytes=48 << 20
        ),
    )(
        values.T,
        gate_inner.T,
        gate_outer.T,
        teacher.T,
        filter_one,
        filter_two,
        w_out.T,
        gene_ids.reshape(1, LANES),
        cell_lengths,
        table,
    )
    return (grads[0].T, grads[1].T, grads[2].T) + tuple(grads[3:])


def solution(mesh):
    blocks, groups = mesh.shape["seq"], mesh.shape["chan"]
    return jax.shard_map(
        functools.partial(per_device, blocks, groups),
        mesh=mesh,
        in_specs=(
            P("seq", "chan"),
            P("seq", "chan"),
            P("seq", "chan"),
            P("chan", "seq"),
            P("chan", "seq"),
            P("seq", "chan"),
            P(None, "chan"),
            P("seq"),
            P(),
            P(),
        ),
        out_specs=(
            P("seq", "chan"),
            P("seq", "chan"),
            P("seq", "chan"),
            P("chan", "seq"),
            P("chan", "seq"),
            P("seq", "chan"),
        ),
        check_vma=False,
    )
```

```python
import functools

import jax
import jax.numpy as jnp
from jax import lax
from jax.experimental import pallas as pl
from jax.experimental.pallas import tpu as pltpu
from jax.sharding import PartitionSpec as P

F32 = jnp.float32
BF16 = jnp.bfloat16
MESH = pl.DeviceIdType.MESH
HIGHEST = lax.Precision.HIGHEST
LANES = 128


def nn(left, right, precision=None):
    return lax.dot_general(
        left, right, (((1,), (0,)), ((), ())), precision=precision, preferred_element_type=F32
    )


def nt(left, right):
    return lax.dot_general(left, right, (((1,), (1,)), ((), ())), preferred_element_type=F32)


def tn(left, right, precision=None):
    return lax.dot_general(
        left, right, (((0,), (0,)), ((), ())), precision=precision, preferred_element_type=F32
    )


def split(value):
    high = value.astype(BF16)
    return high, (value - high.astype(F32)).astype(BF16)


def multiple(index, factor):
    return pl.multiple_of(index * factor, factor)


def kernel(
    blocks,
    groups,
    values,
    gate_inner,
    gate_outer,
    teacher,
    filter_one,
    filter_two,
    w_out,
    gene_ids,
    cell_lengths,
    table,
    out_values,
    out_inner,
    out_outer,
    out_one,
    out_two,
    out_w,
    stage,
    send1,
    recv1,
    flat1,
    pad,
    gate_c,
    conv_c,
    lags_one,
    lags_two,
    back_one,
    back_two,
    wide_one,
    wide_two,
    wide_back,
    toe_one,
    toe_two,
    upper_one,
    upper_two,
    total,
    send2,
    recv2,
    second_t,
    outer_t,
    teach_t,
    w_blocks,
    w_rows,
    token_w,
    pooled_t,
    pooled_all,
    dev_t,
    dev_all,
    gw_send,
    gw_recv,
    send5,
    recv5,
    cross,
    sums,
    flat6,
    send6,
    recv6,
    send_sem,
    recv_sem,
):
    half_count = blocks // 2
    channels = values.shape[0]
    share = channels // half_count
    rows = share * blocks
    own_rows = share * half_count
    row1 = send1.shape[1]
    row6 = send6.shape[1]
    span = wide_one.shape[1] // LANES
    steps = blocks // span
    shift = share * span
    s = lax.axis_index("seq")
    g = lax.axis_index("chan")
    half = lax.div(s, half_count)
    place = lax.rem(s, half_count)

    ring = half_count // 2
    near = [(turn, core) for turn in range(ring) for core in (0, 1)]
    near.sort(key=lambda at: -min(at[0], ring - at[0]))

    def place_at(turn, core):
        return jnp.bitwise_xor(jnp.bitwise_and(place + 2 * turn, half_count - 1), core)

    half_peers = [place_at(turn, core) for turn, core in near if turn or core]
    seq_peers = [(1 - half, place_at(turn, core)) for turn, core in near]
    seq_peers = seq_peers + [(half, peer) for peer in half_peers]
    chan_order = sorted(range(1, groups), key=lambda d: -(min(d // 4, 4 - d // 4) + d % 4))
    chan_peers = [jnp.bitwise_and(g + d, groups - 1) for d in chan_order]

    barrier = pltpu.get_barrier_semaphore()
    for other, peer in seq_peers:
        pl.semaphore_signal(
            barrier, inc=1, device_id={"seq": other * half_count + peer}, device_id_type=MESH
        )
    for peer in chan_peers:
        pl.semaphore_signal(barrier, inc=1, device_id={"chan": peer}, device_id_type=MESH)

    def remote(src, dst, index, device):
        pltpu.make_async_remote_copy(
            src_ref=src,
            dst_ref=dst,
            send_sem=send_sem.at[index],
            recv_sem=recv_sem.at[index],
            device_id=device,
            device_id_type=MESH,
        ).start()

    def to_seq(index, src_of, dst):
        for other, peer in seq_peers:
            remote(src_of(other, peer), dst, index, {"seq": other * half_count + peer})
        pltpu.make_async_copy(src_of(half, place), dst, recv_sem.at[index]).start()

    def to_half(index, src_of, dst):
        for peer in half_peers:
            remote(src_of(peer), dst, index, {"seq": half * half_count + peer})
        pltpu.make_async_copy(src_of(place), dst, recv_sem.at[index]).start()

    def to_chan(index, src_of, dst):
        for peer in chan_peers:
            remote(src_of(peer), dst, index, {"chan": peer})
        pltpu.make_async_copy(src_of(g), dst, recv_sem.at[index]).start()

    def arrived(index, ref):
        pltpu.make_async_copy(ref, ref, recv_sem.at[index]).wait()

    def sent(index, ref):
        pltpu.make_async_copy(ref, ref, send_sem.at[index]).wait()

    values_t = values[...].astype(F32)
    inner_t = gate_inner[...].astype(F32)
    high_one, low_one = split(filter_one[...])
    high_two, low_two = split(filter_two[...])
    filter_rows = jnp.concatenate(
        [high_one.astype(F32), low_one.astype(F32), high_two.astype(F32), low_two.astype(F32)], axis=0
    )
    for p in range(half_count):
        stage[p, 0:share, :] = values_t[p * share : (p + 1) * share]
        stage[p, share : 2 * share, :] = inner_t[p * share : (p + 1) * share]
        stage[p, 2 * share : 2 * share + 4, :] = filter_rows
        if 2 * share + 4 < row1:
            stage[p, 2 * share + 4 : row1, :] = jnp.zeros((row1 - 2 * share - 4, LANES), F32)
    send1[...] = stage[...].astype(BF16)
    pl.semaphore_wait(barrier, blocks + groups - 2)
    to_seq(0, lambda other, peer: send1.at[peer], recv1.at[s])
    to_chan(
        1,
        lambda peer: w_out.at[:, pl.ds(multiple(lax.div(peer, 2), LANES), LANES)],
        w_blocks.at[g],
    )

    outer_t[...] = gate_outer[...].astype(F32)
    teach_t[...] = teacher[...].astype(F32)
    ids = gene_ids[...]
    hot_rows = (
        lax.broadcasted_iota(jnp.int32, (table.shape[0], LANES), 0) == lax.shift_right_logical(ids, 7)
    ).astype(F32)
    picked = tn(table[...], hot_rows, HIGHEST)
    hot_lanes = lax.broadcasted_iota(jnp.int32, (LANES, LANES), 0) == jnp.bitwise_and(ids, 127)
    weight = jnp.sum(jnp.where(hot_lanes, picked, 0.0), axis=0, keepdims=True)
    token = s * LANES + lax.broadcasted_iota(jnp.int32, (1, LANES), 1)
    opening = token == 0
    start = cell_lengths[0]
    for cell in range(1, cell_lengths.shape[0]):
        opening = jnp.logical_or(opening, token == start)
        start = start + cell_lengths[cell]
    token_w[...] = jnp.where(opening, 0.0, weight)
    edge = pad.shape[0] - rows
    edge = edge // 2
    for first in (0, edge + rows):
        pad[first : first + edge, :] = jnp.zeros((edge, LANES), F32)
    empty = jnp.zeros((rows, span * LANES), BF16)
    wide_one[0:rows, :] = empty
    wide_two[0:rows, :] = empty
    wide_back[rows : 2 * rows, :] = empty

    row_iota = lax.broadcasted_iota(jnp.int32, (LANES, LANES), 0)
    lane_iota = lax.broadcasted_iota(jnp.int32, (LANES, LANES), 1)
    flip = (row_iota + lane_iota == LANES - 1).astype(BF16)
    row8 = lax.broadcasted_iota(jnp.int32, (8, LANES), 0)
    lane8 = lax.broadcasted_iota(jnp.int32, (8, LANES), 1)
    tiles = LANES // 8

    def staggered(block, first):
        return pltpu.roll(block, first, axis=1, stride=1, stride_axis=0)

    def turn(block, amount):
        return pltpu.roll(block, amount, axis=1) if amount else block

    def toeplitz_block(row, before, write, upper):
        base = staggered(jnp.broadcast_to(row, (8, LANES)), 1 if upper else 0)
        turned = [turn(base, 8 * j) for j in range(tiles)]
        for j in range(0, tiles, 2):
            pair = []
            for i in (j, j + 1):
                keep = lane8 <= row8 + 8 * i if upper else lane8 >= row8 + 8 * i
                pair.append(jnp.where(keep, turned[i], before[i]))
            high, low = split(jnp.concatenate(pair, axis=0))
            write(8 * j, high, low)
        return turned

    def toeplitz_loop(lags, toe):
        def body(m, before):
            def write(first, high, low):
                at = pl.ds(pl.multiple_of(m * LANES + first, 16), 16)
                toe[at, 0:LANES] = high
                toe[at, LANES : 2 * LANES] = low

            return tuple(toeplitz_block(lags[pl.ds(m, 1), :], before, write, True))

        lax.fori_loop(0, blocks, body, (jnp.zeros((8, LANES), F32),) * tiles)

    def toeplitz_step(lags, toe, step, before):
        for m in range(step * span, (step + 1) * span):

            def write(first, high, low):
                at = slice(m * LANES + first, m * LANES + first + 16)
                toe[at, 0:LANES] = high
                toe[at, LANES : 2 * LANES] = low

            before = toeplitz_block(lags[m : m + 1, :], before, write, False)
        return before

    def weights_of(toe, step):
        return toe[step * span * LANES : (step + 1) * span * LANES, :]

    def joined(product):
        return product[:, 0:LANES] + product[:, LANES : 2 * LANES]

    def widen(wide, first, direction):
        for j in range(span):
            at = edge + direction * share * j
            wide[first : first + rows, j * LANES : (j + 1) * LANES] = pad[at : at + rows, :].astype(BF16)

    own_at = pl.ds(multiple(half, own_rows), own_rows)
    arrived(0, recv1)
    flat1[...] = recv1[...].astype(F32).reshape(blocks * row1, LANES)

    def every(first):
        return flat1[pl.ds(first, blocks, stride=row1), :]

    lags_one[...] = every(2 * share) + every(2 * share + 1)
    lags_two[...] = every(2 * share + 2) + every(2 * share + 3)
    for c in range(share):
        pad[pl.ds(edge + c, blocks, stride=share), :] = every(c)
        gate_c[pl.ds(c, blocks, stride=share), :] = every(share + c)
    widen(wide_one, rows, -1)
    before = [jnp.zeros((8, LANES), F32)] * tiles
    for step in range(steps):
        before = toeplitz_step(lags_one, toe_one, step, before)
        part = nn(wide_one[rows : 2 * rows - shift * step, :], weights_of(toe_one, step))
        if step == 0:
            total[...] = part
        else:
            total[shift * step : rows, :] += part
    first_conv = joined(total[...])
    conv_c[...] = first_conv
    pad[edge : edge + rows, :] = gate_c[...] * first_conv
    widen(wide_two, rows, -1)
    before = [jnp.zeros((8, LANES), F32)] * tiles
    product = jnp.zeros((own_rows, 2 * LANES), F32)
    for step in range(steps):
        before = toeplitz_step(lags_two, toe_two, step, before)
        at = pl.multiple_of(rows + half * own_rows - shift * step, shift)
        product = product + nn(wide_two[pl.ds(at, own_rows), :], weights_of(toe_two, step))
    send2[...] = joined(product).reshape(half_count, share, LANES)
    to_half(2, lambda peer: send2.at[peer], recv2.at[place])

    back_two[...] = nn(every(2 * share + 2).astype(BF16), flip) + nn(every(2 * share + 3).astype(BF16), flip)
    toeplitz_loop(back_two, upper_two)
    arrived(1, w_blocks)
    stacked = w_blocks[...].astype(F32).reshape(groups * channels, LANES)
    w_rows[...] = stacked.T.astype(BF16)

    arrived(2, recv2)
    second_t[...] = recv2[...].reshape(channels, LANES)
    pooled_t[...] = (outer_t[...] * second_t[...]).astype(BF16)
    to_chan(3, lambda peer: pooled_t, pooled_all.at[g])
    back_one[...] = nn(every(2 * share).astype(BF16), flip) + nn(every(2 * share + 1).astype(BF16), flip)
    toeplitz_loop(back_one, upper_one)
    arrived(3, pooled_all)
    width = groups * channels
    pooled = pooled_all[...].reshape(width, LANES)
    output = nn(w_out[...], pooled)
    deviation = (token_w[...] * (output - teach_t[...])).astype(BF16)
    dev_t[...] = deviation
    to_chan(4, lambda peer: dev_t, dev_all.at[g])

    share_w = width // blocks
    half_w = share_w // 2
    parts = pooled.reshape(blocks, 2, half_w, LANES)
    left = jnp.concatenate(
        [parts[:, 0].reshape(blocks * half_w, LANES), parts[:, 1].reshape(blocks * half_w, LANES)], axis=1
    )
    blank = jnp.zeros_like(deviation)
    right = jnp.concatenate(
        [jnp.concatenate([deviation, blank], axis=1), jnp.concatenate([blank, deviation], axis=1)], axis=0
    )
    gw_send[...] = nt(left, right).reshape(blocks, half_w, LANES).astype(gw_send.dtype)
    to_seq(5, lambda other, peer: gw_send.at[other * half_count + peer], gw_recv.at[s])

    arrived(4, dev_all)
    back_outer = nn(
        w_rows[pl.ds(multiple(lax.rem(g, 2), channels), channels), :], dev_all[...].reshape(width, LANES)
    )
    back_second = back_outer * outer_t[...]
    send5[...] = back_second.astype(BF16).reshape(half_count, share, LANES)
    to_seq(6, lambda other, peer: send5.at[peer], recv5.at[s])
    out_outer[...] = (back_outer * second_t[...]).astype(BF16)

    arrived(6, recv5)
    signal = recv5[...].astype(F32).reshape(rows, LANES)
    pad[edge : edge + rows, :] = signal
    widen(wide_back, 0, 1)
    for step in range(steps):
        part = nn(wide_back[shift * step : rows, :], weights_of(upper_two, step))
        if step == 0:
            total[...] = part
        else:
            total[0 : rows - shift * step, :] += part
    back_inner = joined(total[...])
    back_first = back_inner * gate_c[...]
    pad[edge : edge + rows, :] = back_first
    conv_c[...] = back_inner * conv_c[...]
    widen(wide_back, 0, 1)
    product = jnp.zeros((own_rows, 2 * LANES), F32)
    for step in range(steps):
        at = pl.multiple_of(half * own_rows + shift * step, shift)
        product = product + nn(wide_back[pl.ds(at, own_rows), :], weights_of(upper_one, step))
    grad_values_c = joined(product)
    grad_inner_c = conv_c[own_at, :]
    for p in range(half_count):
        at = slice(p * share, (p + 1) * share)
        flat6[p * row6 : p * row6 + share, :] = grad_values_c[at]
        flat6[p * row6 + share : p * row6 + 2 * share, :] = grad_inner_c[at]

    def filter_grad(back, wide, column):
        turned = nt(flip, back.astype(BF16)).astype(BF16)
        for j in range(half_count // span):
            at = pl.multiple_of(rows - half * own_rows - shift * j, shift)
            cross[:, j * span * LANES : (j + 1) * span * LANES] = nn(turned, wide[pl.ds(at, rows), :])
        at = multiple(1 - half, own_rows)
        cross[:, half_count * LANES : (half_count + 1) * LANES] = nn(turned, wide[pl.ds(at, rows), 0:LANES])

        def block(m):
            return [
                turn(cross[8 * j : 8 * j + 8, m * LANES : (m + 1) * LANES], 8 * j) for j in range(tiles)
            ]

        def added(terms):
            while len(terms) > 1:
                terms = [a + b for a, b in zip(terms[::2], terms[1::2])]
            return terms[0]

        later = block(half_count)
        later = staggered(added([jnp.where(lane8 >= 8 * j, later[j], 0.0) for j in range(tiles)]), 0), later
        for m in range(half_count - 1, -1, -1):
            after_sum, after = later
            current = block(m)
            here = staggered(
                added([jnp.where(lane8 >= 8 * j, current[j], after[j]) for j in range(tiles)]), 0
            )
            sums[m : m + 1, :] = jnp.sum(jnp.where(lane8 >= row8, here, after_sum), axis=0, keepdims=True)
            later = here, current
        high, low = split(sums[...])
        flat6[pl.ds(column, half_count, stride=row6), :] = high.astype(F32)
        flat6[pl.ds(column + 1, half_count, stride=row6), :] = low.astype(F32)

    filter_grad(signal, wide_two, 2 * share + 2)
    filter_grad(back_first, wide_one, 2 * share)
    for c in range(2 * share + 4, row6):
        flat6[pl.ds(c, half_count, stride=row6), :] = jnp.zeros((half_count, LANES), F32)
    send6[...] = flat6[...].reshape(half_count, row6, LANES).astype(BF16)
    to_half(7, lambda peer: send6.at[peer], recv6.at[place])

    arrived(5, gw_recv)
    total_w = jnp.sum(gw_recv[...].astype(F32), axis=0)
    out_w[0:half_w, :] = total_w[:, 0:channels]
    out_w[half_w:share_w, :] = total_w[:, channels : 2 * channels]

    sent(0, recv1.at[pl.ds(0, blocks - 1)])
    sent(1, w_blocks.at[pl.ds(0, groups - 1)])
    sent(2, recv2.at[pl.ds(0, half_count - 1)])
    sent(3, pooled_all.at[pl.ds(0, groups - 1)])
    sent(4, dev_all.at[pl.ds(0, groups - 1)])
    sent(5, gw_recv.at[pl.ds(0, blocks - 1)])
    sent(6, recv5.at[pl.ds(0, blocks - 1)])
    arrived(7, recv6)
    flat6[...] = recv6[...].astype(F32).reshape(half_count * row6, LANES)
    for p in range(half_count):
        at = slice(p * share, (p + 1) * share)
        second_t[at, :] = flat6[p * row6 : p * row6 + share, :]
        outer_t[at, :] = flat6[p * row6 + share : p * row6 + 2 * share, :]
    out_values[...] = second_t[...].astype(BF16)
    out_inner[...] = outer_t[...].astype(BF16)
    lag_rows = []
    for column in (2 * share, 2 * share + 2):
        both = flat6[pl.ds(column, half_count, stride=row6), :] + flat6[
            pl.ds(column + 1, half_count, stride=row6), :
        ]
        lag_rows.append(jnp.sum(both, axis=0, keepdims=True))
    lag_rows.append(jnp.zeros((6, LANES), F32))
    ordered = nn(jnp.concatenate(lag_rows, axis=0), flip.astype(F32), HIGHEST)
    out_one[...] = ordered[0:1]
    out_two[...] = ordered[1:2]
    sent(7, recv6.at[pl.ds(0, half_count - 1)])


def hand_on(*refs):
    count = len(refs) // 2
    for source, target in zip(refs[:count], refs[count:]):
        target[...] = source[...]


def rounded(count, factor):
    return -(-count // factor) * factor


def per_device(
    blocks,
    groups,
    values,
    gate_inner,
    gate_outer,
    filter_one,
    filter_two,
    teacher,
    w_out,
    gene_ids,
    cell_lengths,
    gene_weights,
):
    length, channels = values.shape
    half_count = blocks // 2
    share = channels // half_count
    rows = share * blocks
    width = groups * channels
    share_w = width // blocks
    row1 = rounded(2 * share + 4, 16)
    span = max(1, 16 // share)
    vocab = gene_weights.shape[0]
    padded = rounded(vocab, 8 * LANES)
    table = jnp.pad(gene_weights, (0, padded - vocab)).reshape(padded // LANES, LANES)
    vmem = pl.BlockSpec(memory_space=pltpu.VMEM)
    smem = pl.BlockSpec(memory_space=pltpu.SMEM)
    V = pltpu.VMEM
    grads = pl.pallas_call(
        functools.partial(kernel, blocks, groups),
        out_shape=(
            jax.ShapeDtypeStruct((channels, length), BF16),
            jax.ShapeDtypeStruct((channels, length), BF16),
            jax.ShapeDtypeStruct((channels, length), BF16),
            jax.ShapeDtypeStruct((1, LANES), F32),
            jax.ShapeDtypeStruct((1, LANES), F32),
            jax.ShapeDtypeStruct((share_w, channels), F32),
        ),
        in_specs=[vmem] * 8 + [smem, vmem],
        out_specs=(vmem,) * 6,
        scratch_shapes=[
            V((half_count, row1, LANES), F32),
            V((half_count, row1, LANES), BF16),
            V((blocks, row1, LANES), BF16),
            V((blocks * row1, LANES), F32),
            V((rows + 32, LANES), F32),
            V((rows, LANES), F32),
            V((rows, LANES), F32),
            V((blocks, LANES), F32),
            V((blocks, LANES), F32),
            V((blocks, LANES), F32),
            V((blocks, LANES), F32),
            V((2 * rows, span * LANES), BF16),
            V((2 * rows, span * LANES), BF16),
            V((2 * rows, span * LANES), BF16),
            V((blocks * LANES, 2 * LANES), BF16),
            V((blocks * LANES, 2 * LANES), BF16),
            V((blocks * LANES, 2 * LANES), BF16),
            V((blocks * LANES, 2 * LANES), BF16),
            V((rows, 2 * LANES), F32),
            V((half_count, share, LANES), F32),
            V((half_count, share, LANES), F32),
            V((channels, LANES), F32),
            V((channels, LANES), F32),
            V((channels, LANES), F32),
            V((groups, channels, LANES), BF16),
            V((LANES, width), BF16),
            V((1, LANES), F32),
            V((channels, LANES), BF16),
            V((groups, channels, LANES), BF16),
            V((channels, LANES), BF16),
            V((groups, channels, LANES), BF16),
            V((blocks, share_w // 2, LANES), BF16),
            V((blocks, share_w // 2, LANES), BF16),
            V((half_count, share, LANES), BF16),
            V((blocks, share, LANES), BF16),
            V((LANES, (half_count + 1) * LANES), F32),
            V((half_count, LANES), F32),
            V((half_count * row1, LANES), F32),
            V((half_count, row1, LANES), BF16),
            V((half_count, row1, LANES), BF16),
            pltpu.SemaphoreType.DMA((8,)),
            pltpu.SemaphoreType.DMA((8,)),
        ],
        compiler_params=pltpu.CompilerParams(
            collective_id=0, has_side_effects=True, vmem_limit_bytes=48 << 20
        ),
    )(
        values.T,
        gate_inner.T,
        gate_outer.T,
        teacher.T,
        filter_one,
        filter_two,
        w_out.T,
        gene_ids.reshape(1, LANES),
        cell_lengths,
        table,
    )
    grads = pl.pallas_call(
        hand_on,
        out_shape=tuple(jax.ShapeDtypeStruct(grad.shape, grad.dtype) for grad in grads),
        in_specs=[vmem] * 6,
        out_specs=(vmem,) * 6,
        compiler_params=pltpu.CompilerParams(vmem_limit_bytes=1 << 20),
    )(*grads)
    return (grads[0].T, grads[1].T, grads[2].T) + tuple(grads[3:])


def solution(mesh):
    blocks, groups = mesh.shape["seq"], mesh.shape["chan"]
    return jax.shard_map(
        functools.partial(per_device, blocks, groups),
        mesh=mesh,
        in_specs=(
            P("seq", "chan"),
            P("seq", "chan"),
            P("seq", "chan"),
            P("chan", "seq"),
            P("chan", "seq"),
            P("seq", "chan"),
            P(None, "chan"),
            P("seq"),
            P(),
            P(),
        ),
        out_specs=(
            P("seq", "chan"),
            P("seq", "chan"),
            P("seq", "chan"),
            P("chan", "seq"),
            P("chan", "seq"),
            P("seq", "chan"),
        ),
        check_vma=False,
    )
```

```python
import functools

import jax
import jax.numpy as jnp
from jax import lax
from jax.experimental import pallas as pl
from jax.experimental.pallas import tpu as pltpu
from jax.sharding import PartitionSpec as P

F32 = jnp.float32
BF16 = jnp.bfloat16
MESH = pl.DeviceIdType.MESH
HIGHEST = lax.Precision.HIGHEST
LANES = 128


def nn(left, right, precision=None):
    return lax.dot_general(
        left, right, (((1,), (0,)), ((), ())), precision=precision, preferred_element_type=F32
    )


def nt(left, right):
    return lax.dot_general(left, right, (((1,), (1,)), ((), ())), preferred_element_type=F32)


def tn(left, right, precision=None):
    return lax.dot_general(
        left, right, (((0,), (0,)), ((), ())), precision=precision, preferred_element_type=F32
    )


def split(value):
    high = value.astype(BF16)
    return high, (value - high.astype(F32)).astype(BF16)


def multiple(index, factor):
    return pl.multiple_of(index * factor, factor)


def kernel(
    blocks,
    groups,
    values,
    gate_inner,
    gate_outer,
    teacher,
    filter_one,
    filter_two,
    w_out,
    gene_ids,
    cell_lengths,
    gene_weights,
    out_values,
    out_inner,
    out_outer,
    out_one,
    out_two,
    out_w,
    stage,
    send1,
    recv1,
    flat1,
    pad,
    gate_c,
    conv_c,
    lags_one,
    lags_two,
    back_one,
    back_two,
    wide_one,
    wide_two,
    wide_back,
    toe_one,
    toe_two,
    upper_one,
    upper_two,
    total,
    send2,
    recv2,
    second_t,
    outer_t,
    teach_t,
    w_blocks,
    w_rows,
    token_w,
    table,
    pooled_t,
    pooled_all,
    dev_t,
    dev_all,
    gw_send,
    gw_recv,
    send5,
    recv5,
    cross,
    sums,
    flat6,
    send6,
    recv6,
    send_sem,
    recv_sem,
):
    half_count = blocks // 2
    channels = values.shape[0]
    share = channels // half_count
    rows = share * blocks
    own_rows = share * half_count
    row1 = send1.shape[1]
    row6 = send6.shape[1]
    span = wide_one.shape[1] // LANES
    steps = blocks // span
    shift = share * span
    s = lax.axis_index("seq")
    g = lax.axis_index("chan")
    half = lax.div(s, half_count)
    place = lax.rem(s, half_count)

    ring = half_count // 2
    near = [(turn, core) for turn in range(ring) for core in (0, 1)]
    near.sort(key=lambda at: -min(at[0], ring - at[0]))

    def place_at(turn, core):
        return jnp.bitwise_xor(jnp.bitwise_and(place + 2 * turn, half_count - 1), core)

    half_peers = [place_at(turn, core) for turn, core in near if turn or core]
    seq_peers = [(1 - half, place_at(turn, core)) for turn, core in near]
    seq_peers = seq_peers + [(half, peer) for peer in half_peers]
    chan_order = sorted(range(1, groups), key=lambda d: -(min(d // 4, 4 - d // 4) + d % 4))
    chan_peers = [jnp.bitwise_and(g + d, groups - 1) for d in chan_order]

    barrier = pltpu.get_barrier_semaphore()
    for other, peer in seq_peers:
        pl.semaphore_signal(
            barrier, inc=1, device_id={"seq": other * half_count + peer}, device_id_type=MESH
        )
    for peer in chan_peers:
        pl.semaphore_signal(barrier, inc=1, device_id={"chan": peer}, device_id_type=MESH)

    def remote(src, dst, index, device):
        pltpu.make_async_remote_copy(
            src_ref=src,
            dst_ref=dst,
            send_sem=send_sem.at[index],
            recv_sem=recv_sem.at[index],
            device_id=device,
            device_id_type=MESH,
        ).start()

    def to_seq(index, src_of, dst):
        for other, peer in seq_peers:
            remote(src_of(other, peer), dst, index, {"seq": other * half_count + peer})
        pltpu.make_async_copy(src_of(half, place), dst, recv_sem.at[index]).start()

    def to_half(index, src_of, dst):
        for peer in half_peers:
            remote(src_of(peer), dst, index, {"seq": half * half_count + peer})
        pltpu.make_async_copy(src_of(place), dst, recv_sem.at[index]).start()

    def to_chan(index, src_of, dst):
        for peer in chan_peers:
            remote(src_of(peer), dst, index, {"chan": peer})
        pltpu.make_async_copy(src_of(g), dst, recv_sem.at[index]).start()

    def arrived(index, ref):
        pltpu.make_async_copy(ref, ref, recv_sem.at[index]).wait()

    def sent(index, ref):
        pltpu.make_async_copy(ref, ref, send_sem.at[index]).wait()

    values_t = values[...].astype(F32)
    inner_t = gate_inner[...].astype(F32)
    high_one, low_one = split(filter_one[...])
    high_two, low_two = split(filter_two[...])
    filter_rows = jnp.concatenate(
        [high_one.astype(F32), low_one.astype(F32), high_two.astype(F32), low_two.astype(F32)], axis=0
    )
    for p in range(half_count):
        stage[p, 0:share, :] = values_t[p * share : (p + 1) * share]
        stage[p, share : 2 * share, :] = inner_t[p * share : (p + 1) * share]
        stage[p, 2 * share : 2 * share + 4, :] = filter_rows
        if 2 * share + 4 < row1:
            stage[p, 2 * share + 4 : row1, :] = jnp.zeros((row1 - 2 * share - 4, LANES), F32)
    send1[...] = stage[...].astype(BF16)
    pl.semaphore_wait(barrier, blocks + groups - 2)
    to_seq(0, lambda other, peer: send1.at[peer], recv1.at[s])

    outer_t[...] = gate_outer[...].astype(F32)
    teach_t[...] = teacher[...].astype(F32)
    vocab = gene_weights.shape[0]
    whole = vocab // LANES
    table[whole - whole % 8 :, :] = jnp.zeros((table.shape[0] - whole + whole % 8, LANES), F32)
    for line in range(whole):
        table[line : line + 1, :] = gene_weights[pl.ds(line * LANES, LANES)].reshape(1, LANES)
    if vocab % LANES:
        rest = gene_weights[pl.ds(whole * LANES, vocab % LANES)].reshape(1, vocab % LANES)
        table[whole : whole + 1, 0 : vocab % LANES] = rest
    ids = gene_ids[...]
    hot_rows = (
        lax.broadcasted_iota(jnp.int32, (table.shape[0], LANES), 0) == lax.shift_right_logical(ids, 7)
    ).astype(F32)
    picked = tn(table[...], hot_rows, HIGHEST)
    hot_lanes = lax.broadcasted_iota(jnp.int32, (LANES, LANES), 0) == jnp.bitwise_and(ids, 127)
    weight = jnp.sum(jnp.where(hot_lanes, picked, 0.0), axis=0, keepdims=True)
    token = s * LANES + lax.broadcasted_iota(jnp.int32, (1, LANES), 1)
    opening = token == 0
    start = cell_lengths[0]
    for cell in range(1, cell_lengths.shape[0]):
        opening = jnp.logical_or(opening, token == start)
        start = start + cell_lengths[cell]
    token_w[...] = jnp.where(opening, 0.0, weight)
    edge = pad.shape[0] - rows
    edge = edge // 2
    for first in (0, edge + rows):
        pad[first : first + edge, :] = jnp.zeros((edge, LANES), F32)
    empty = jnp.zeros((rows, span * LANES), BF16)
    wide_one[0:rows, :] = empty
    wide_two[0:rows, :] = empty
    wide_back[rows : 2 * rows, :] = empty

    row_iota = lax.broadcasted_iota(jnp.int32, (LANES, LANES), 0)
    lane_iota = lax.broadcasted_iota(jnp.int32, (LANES, LANES), 1)
    flip = (row_iota + lane_iota == LANES - 1).astype(BF16)
    row8 = lax.broadcasted_iota(jnp.int32, (8, LANES), 0)
    lane8 = lax.broadcasted_iota(jnp.int32, (8, LANES), 1)
    tiles = LANES // 8

    def staggered(block, first):
        return pltpu.roll(block, first, axis=1, stride=1, stride_axis=0)

    def turn(block, amount):
        return pltpu.roll(block, amount, axis=1) if amount else block

    def toeplitz_block(row, before, write, upper):
        base = staggered(jnp.broadcast_to(row, (8, LANES)), 1 if upper else 0)
        turned = [turn(base, 8 * j) for j in range(tiles)]
        for j in range(0, tiles, 2):
            pair = []
            for i in (j, j + 1):
                keep = lane8 <= row8 + 8 * i if upper else lane8 >= row8 + 8 * i
                pair.append(jnp.where(keep, turned[i], before[i]))
            high, low = split(jnp.concatenate(pair, axis=0))
            write(8 * j, high, low)
        return turned

    def toeplitz_loop(lags, toe):
        def body(m, before):
            def write(first, high, low):
                at = pl.ds(pl.multiple_of(m * LANES + first, 16), 16)
                toe[at, 0:LANES] = high
                toe[at, LANES : 2 * LANES] = low

            return tuple(toeplitz_block(lags[pl.ds(m, 1), :], before, write, True))

        lax.fori_loop(0, blocks, body, (jnp.zeros((8, LANES), F32),) * tiles)

    def toeplitz_step(lags, toe, step, before):
        for m in range(step * span, (step + 1) * span):

            def write(first, high, low):
                at = slice(m * LANES + first, m * LANES + first + 16)
                toe[at, 0:LANES] = high
                toe[at, LANES : 2 * LANES] = low

            before = toeplitz_block(lags[m : m + 1, :], before, write, False)
        return before

    def weights_of(toe, step):
        return toe[step * span * LANES : (step + 1) * span * LANES, :]

    def joined(product):
        return product[:, 0:LANES] + product[:, LANES : 2 * LANES]

    def widen(wide, first, direction):
        for j in range(span):
            at = edge + direction * share * j
            wide[first : first + rows, j * LANES : (j + 1) * LANES] = pad[at : at + rows, :].astype(BF16)

    own_at = pl.ds(multiple(half, own_rows), own_rows)
    arrived(0, recv1)
    to_chan(
        1,
        lambda peer: w_out.at[:, pl.ds(multiple(lax.div(peer, 2), LANES), LANES)],
        w_blocks.at[g],
    )
    flat1[...] = recv1[...].astype(F32).reshape(blocks * row1, LANES)

    def every(first):
        return flat1[pl.ds(first, blocks, stride=row1), :]

    lags_one[...] = every(2 * share) + every(2 * share + 1)
    lags_two[...] = every(2 * share + 2) + every(2 * share + 3)
    for c in range(share):
        pad[pl.ds(edge + c, blocks, stride=share), :] = every(c)
        gate_c[pl.ds(c, blocks, stride=share), :] = every(share + c)
    widen(wide_one, rows, -1)
    before = [jnp.zeros((8, LANES), F32)] * tiles
    for step in range(steps):
        before = toeplitz_step(lags_one, toe_one, step, before)
        part = nn(wide_one[rows : 2 * rows - shift * step, :], weights_of(toe_one, step))
        if step == 0:
            total[...] = part
        else:
            total[shift * step : rows, :] += part
    first_conv = joined(total[...])
    conv_c[...] = first_conv
    pad[edge : edge + rows, :] = gate_c[...] * first_conv
    widen(wide_two, rows, -1)
    before = [jnp.zeros((8, LANES), F32)] * tiles
    product = jnp.zeros((own_rows, 2 * LANES), F32)
    for step in range(steps):
        before = toeplitz_step(lags_two, toe_two, step, before)
        at = pl.multiple_of(rows + half * own_rows - shift * step, shift)
        product = product + nn(wide_two[pl.ds(at, own_rows), :], weights_of(toe_two, step))
    send2[...] = joined(product).reshape(half_count, share, LANES)
    to_half(2, lambda peer: send2.at[peer], recv2.at[place])

    back_two[...] = nn(every(2 * share + 2).astype(BF16), flip) + nn(every(2 * share + 3).astype(BF16), flip)
    toeplitz_loop(back_two, upper_two)
    arrived(1, w_blocks)
    stacked = w_blocks[...].astype(F32).reshape(groups * channels, LANES)
    w_rows[...] = stacked.T.astype(BF16)

    arrived(2, recv2)
    second_t[...] = recv2[...].reshape(channels, LANES)
    pooled_t[...] = (outer_t[...] * second_t[...]).astype(BF16)
    to_chan(3, lambda peer: pooled_t, pooled_all.at[g])
    back_one[...] = nn(every(2 * share).astype(BF16), flip) + nn(every(2 * share + 1).astype(BF16), flip)
    toeplitz_loop(back_one, upper_one)
    arrived(3, pooled_all)
    width = groups * channels
    pooled = pooled_all[...].reshape(width, LANES)
    output = nn(w_out[...], pooled)
    deviation = (token_w[...] * (output - teach_t[...])).astype(BF16)
    dev_t[...] = deviation
    to_chan(4, lambda peer: dev_t, dev_all.at[g])

    share_w = width // blocks
    half_w = share_w // 2
    parts = pooled.reshape(blocks, 2, half_w, LANES)
    left = jnp.concatenate(
        [parts[:, 0].reshape(blocks * half_w, LANES), parts[:, 1].reshape(blocks * half_w, LANES)], axis=1
    )
    blank = jnp.zeros_like(deviation)
    right = jnp.concatenate(
        [jnp.concatenate([deviation, blank], axis=1), jnp.concatenate([blank, deviation], axis=1)], axis=0
    )
    gw_send[...] = nt(left, right).reshape(blocks, half_w, LANES).astype(gw_send.dtype)

    arrived(4, dev_all)
    back_outer = nn(
        w_rows[pl.ds(multiple(lax.rem(g, 2), channels), channels), :], dev_all[...].reshape(width, LANES)
    )
    back_second = back_outer * outer_t[...]
    send5[...] = back_second.astype(BF16).reshape(half_count, share, LANES)
    to_seq(6, lambda other, peer: send5.at[peer], recv5.at[s])
    to_seq(5, lambda other, peer: gw_send.at[other * half_count + peer], gw_recv.at[s])
    out_outer[...] = (back_outer * second_t[...]).astype(BF16)

    arrived(6, recv5)
    signal = recv5[...].astype(F32).reshape(rows, LANES)
    pad[edge : edge + rows, :] = signal
    widen(wide_back, 0, 1)
    for step in range(steps):
        part = nn(wide_back[shift * step : rows, :], weights_of(upper_two, step))
        if step == 0:
            total[...] = part
        else:
            total[0 : rows - shift * step, :] += part
    back_inner = joined(total[...])
    back_first = back_inner * gate_c[...]
    pad[edge : edge + rows, :] = back_first
    conv_c[...] = back_inner * conv_c[...]
    widen(wide_back, 0, 1)
    product = jnp.zeros((own_rows, 2 * LANES), F32)
    for step in range(steps):
        at = pl.multiple_of(half * own_rows + shift * step, shift)
        product = product + nn(wide_back[pl.ds(at, own_rows), :], weights_of(upper_one, step))
    grad_values_c = joined(product)
    grad_inner_c = conv_c[own_at, :]
    for p in range(half_count):
        at = slice(p * share, (p + 1) * share)
        flat6[p * row6 : p * row6 + share, :] = grad_values_c[at]
        flat6[p * row6 + share : p * row6 + 2 * share, :] = grad_inner_c[at]

    def filter_grad(back, wide, column):
        turned = nt(flip, back.astype(BF16)).astype(BF16)
        for j in range(half_count // span):
            at = pl.multiple_of(rows - half * own_rows - shift * j, shift)
            cross[:, j * span * LANES : (j + 1) * span * LANES] = nn(turned, wide[pl.ds(at, rows), :])
        at = multiple(1 - half, own_rows)
        cross[:, half_count * LANES : (half_count + 1) * LANES] = nn(turned, wide[pl.ds(at, rows), 0:LANES])

        def block(m):
            return [
                turn(cross[8 * j : 8 * j + 8, m * LANES : (m + 1) * LANES], 8 * j) for j in range(tiles)
            ]

        def added(terms):
            while len(terms) > 1:
                terms = [a + b for a, b in zip(terms[::2], terms[1::2])]
            return terms[0]

        later = block(half_count)
        later = staggered(added([jnp.where(lane8 >= 8 * j, later[j], 0.0) for j in range(tiles)]), 0), later
        for m in range(half_count - 1, -1, -1):
            after_sum, after = later
            current = block(m)
            here = staggered(
                added([jnp.where(lane8 >= 8 * j, current[j], after[j]) for j in range(tiles)]), 0
            )
            sums[m : m + 1, :] = jnp.sum(jnp.where(lane8 >= row8, here, after_sum), axis=0, keepdims=True)
            later = here, current
        high, low = split(sums[...])
        flat6[pl.ds(column, half_count, stride=row6), :] = high.astype(F32)
        flat6[pl.ds(column + 1, half_count, stride=row6), :] = low.astype(F32)

    filter_grad(signal, wide_two, 2 * share + 2)
    filter_grad(back_first, wide_one, 2 * share)
    for c in range(2 * share + 4, row6):
        flat6[pl.ds(c, half_count, stride=row6), :] = jnp.zeros((half_count, LANES), F32)
    send6[...] = flat6[...].reshape(half_count, row6, LANES).astype(BF16)
    to_half(7, lambda peer: send6.at[peer], recv6.at[place])

    arrived(5, gw_recv)
    total_w = jnp.sum(gw_recv[...].astype(F32), axis=0)
    out_w[0:half_w, :] = total_w[:, 0:channels]
    out_w[half_w:share_w, :] = total_w[:, channels : 2 * channels]

    sent(0, recv1.at[pl.ds(0, blocks - 1)])
    sent(1, w_blocks.at[pl.ds(0, groups - 1)])
    sent(2, recv2.at[pl.ds(0, half_count - 1)])
    sent(3, pooled_all.at[pl.ds(0, groups - 1)])
    sent(4, dev_all.at[pl.ds(0, groups - 1)])
    sent(5, gw_recv.at[pl.ds(0, blocks - 1)])
    sent(6, recv5.at[pl.ds(0, blocks - 1)])
    arrived(7, recv6)
    flat6[...] = recv6[...].astype(F32).reshape(half_count * row6, LANES)
    for p in range(half_count):
        at = slice(p * share, (p + 1) * share)
        second_t[at, :] = flat6[p * row6 : p * row6 + share, :]
        outer_t[at, :] = flat6[p * row6 + share : p * row6 + 2 * share, :]
    out_values[...] = second_t[...].astype(BF16)
    out_inner[...] = outer_t[...].astype(BF16)
    lag_rows = []
    for column in (2 * share, 2 * share + 2):
        both = flat6[pl.ds(column, half_count, stride=row6), :] + flat6[
            pl.ds(column + 1, half_count, stride=row6), :
        ]
        lag_rows.append(jnp.sum(both, axis=0, keepdims=True))
    lag_rows.append(jnp.zeros((6, LANES), F32))
    ordered = nn(jnp.concatenate(lag_rows, axis=0), flip.astype(F32), HIGHEST)
    out_one[...] = ordered[0:1]
    out_two[...] = ordered[1:2]
    sent(7, recv6.at[pl.ds(0, half_count - 1)])


def hand_on(*refs):
    count = len(refs) // 2
    for source, target in zip(refs[:count], refs[count:]):
        target[...] = source[...]


def rounded(count, factor):
    return -(-count // factor) * factor


def per_device(
    blocks,
    groups,
    values,
    gate_inner,
    gate_outer,
    filter_one,
    filter_two,
    teacher,
    w_out,
    gene_ids,
    cell_lengths,
    gene_weights,
):
    length, channels = values.shape
    half_count = blocks // 2
    share = channels // half_count
    rows = share * blocks
    width = groups * channels
    share_w = width // blocks
    row1 = rounded(2 * share + 4, 16)
    span = max(1, 16 // share)
    vocab = gene_weights.shape[0]
    vmem = pl.BlockSpec(memory_space=pltpu.VMEM)
    smem = pl.BlockSpec(memory_space=pltpu.SMEM)
    V = pltpu.VMEM
    grads = pl.pallas_call(
        functools.partial(kernel, blocks, groups),
        out_shape=(
            jax.ShapeDtypeStruct((channels, length), BF16),
            jax.ShapeDtypeStruct((channels, length), BF16),
            jax.ShapeDtypeStruct((channels, length), BF16),
            jax.ShapeDtypeStruct((1, LANES), F32),
            jax.ShapeDtypeStruct((1, LANES), F32),
            jax.ShapeDtypeStruct((share_w, channels), F32),
        ),
        in_specs=[vmem] * 8 + [smem, vmem],
        out_specs=(vmem,) * 6,
        scratch_shapes=[
            V((half_count, row1, LANES), F32),
            V((half_count, row1, LANES), BF16),
            V((blocks, row1, LANES), BF16),
            V((blocks * row1, LANES), F32),
            V((rows + 32, LANES), F32),
            V((rows, LANES), F32),
            V((rows, LANES), F32),
            V((blocks, LANES), F32),
            V((blocks, LANES), F32),
            V((blocks, LANES), F32),
            V((blocks, LANES), F32),
            V((2 * rows, span * LANES), BF16),
            V((2 * rows, span * LANES), BF16),
            V((2 * rows, span * LANES), BF16),
            V((blocks * LANES, 2 * LANES), BF16),
            V((blocks * LANES, 2 * LANES), BF16),
            V((blocks * LANES, 2 * LANES), BF16),
            V((blocks * LANES, 2 * LANES), BF16),
            V((rows, 2 * LANES), F32),
            V((half_count, share, LANES), F32),
            V((half_count, share, LANES), F32),
            V((channels, LANES), F32),
            V((channels, LANES), F32),
            V((channels, LANES), F32),
            V((groups, channels, LANES), BF16),
            V((LANES, width), BF16),
            V((1, LANES), F32),
            V((rounded(vocab, 8 * LANES) // LANES, LANES), F32),
            V((channels, LANES), BF16),
            V((groups, channels, LANES), BF16),
            V((channels, LANES), BF16),
            V((groups, channels, LANES), BF16),
            V((blocks, share_w // 2, LANES), BF16),
            V((blocks, share_w // 2, LANES), BF16),
            V((half_count, share, LANES), BF16),
            V((blocks, share, LANES), BF16),
            V((LANES, (half_count + 1) * LANES), F32),
            V((half_count, LANES), F32),
            V((half_count * row1, LANES), F32),
            V((half_count, row1, LANES), BF16),
            V((half_count, row1, LANES), BF16),
            pltpu.SemaphoreType.DMA((8,)),
            pltpu.SemaphoreType.DMA((8,)),
        ],
        compiler_params=pltpu.CompilerParams(
            collective_id=0, has_side_effects=True, vmem_limit_bytes=48 << 20
        ),
    )(
        values.T,
        gate_inner.T,
        gate_outer.T,
        teacher.T,
        filter_one,
        filter_two,
        w_out.T,
        gene_ids.reshape(1, LANES),
        cell_lengths,
        gene_weights,
    )
    grads = pl.pallas_call(
        hand_on,
        out_shape=tuple(jax.ShapeDtypeStruct(grad.shape, grad.dtype) for grad in grads),
        in_specs=[vmem] * 6,
        out_specs=(vmem,) * 6,
        compiler_params=pltpu.CompilerParams(vmem_limit_bytes=1 << 20),
    )(*grads)
    return (grads[0].T, grads[1].T, grads[2].T) + tuple(grads[3:])


def solution(mesh):
    blocks, groups = mesh.shape["seq"], mesh.shape["chan"]
    return jax.shard_map(
        functools.partial(per_device, blocks, groups),
        mesh=mesh,
        in_specs=(
            P("seq", "chan"),
            P("seq", "chan"),
            P("seq", "chan"),
            P("chan", "seq"),
            P("chan", "seq"),
            P("seq", "chan"),
            P(None, "chan"),
            P("seq"),
            P(),
            P(),
        ),
        out_specs=(
            P("seq", "chan"),
            P("seq", "chan"),
            P("seq", "chan"),
            P("chan", "seq"),
            P("chan", "seq"),
            P("seq", "chan"),
        ),
        check_vma=False,
    )
```

```python
import functools

import jax
import jax.numpy as jnp
from jax import lax
from jax.experimental import pallas as pl
from jax.experimental.pallas import tpu as pltpu
from jax.sharding import PartitionSpec as P

F32 = jnp.float32
BF16 = jnp.bfloat16
MESH = pl.DeviceIdType.MESH
HIGHEST = lax.Precision.HIGHEST
LANES = 128


def nn(left, right, precision=None):
    return lax.dot_general(
        left, right, (((1,), (0,)), ((), ())), precision=precision, preferred_element_type=F32
    )


def nt(left, right):
    return lax.dot_general(left, right, (((1,), (1,)), ((), ())), preferred_element_type=F32)


def tn(left, right, precision=None):
    return lax.dot_general(
        left, right, (((0,), (0,)), ((), ())), precision=precision, preferred_element_type=F32
    )


def split(value):
    high = value.astype(BF16)
    return high, (value - high.astype(F32)).astype(BF16)


def multiple(index, factor):
    return pl.multiple_of(index * factor, factor)


def kernel(
    blocks,
    groups,
    values_in,
    inner_in,
    outer_in,
    teacher_in,
    one_in,
    two_in,
    w_in,
    ids_in,
    lengths_in,
    weights_in,
    out_values,
    out_inner,
    out_outer,
    out_one,
    out_two,
    out_w,
    values,
    gate_inner,
    gate_outer,
    teacher,
    filter_one,
    filter_two,
    w_out,
    gene_ids,
    cell_lengths,
    gene_weights,
    stage,
    send1,
    recv1,
    flat1,
    pad,
    gate_c,
    conv_c,
    lags_one,
    lags_two,
    back_one,
    back_two,
    wide_one,
    wide_two,
    wide_back,
    toe_one,
    toe_two,
    upper_one,
    upper_two,
    total,
    send2,
    recv2,
    second_t,
    outer_t,
    teach_t,
    w_blocks,
    w_rows,
    token_w,
    table,
    pooled_t,
    pooled_all,
    dev_t,
    dev_all,
    gw_send,
    gw_recv,
    send5,
    recv5,
    cross,
    sums,
    flat6,
    send6,
    recv6,
    send_sem,
    recv_sem,
    fetch_sem,
):
    fetches = [
        pltpu.make_async_copy(source, target, fetch_sem.at[index])
        for index, (source, target) in enumerate(
            [
                (values_in, values),
                (inner_in, gate_inner),
                (one_in, filter_one),
                (two_in, filter_two),
                (outer_in, gate_outer),
                (teacher_in, teacher),
                (ids_in, gene_ids),
                (lengths_in, cell_lengths),
                (weights_in, gene_weights),
                (w_in, w_out),
            ]
        )
    ]
    for fetch in fetches:
        fetch.start()
    half_count = blocks // 2
    channels = values.shape[0]
    share = channels // half_count
    rows = share * blocks
    own_rows = share * half_count
    row1 = send1.shape[1]
    row6 = send6.shape[1]
    span = wide_one.shape[1] // LANES
    steps = blocks // span
    shift = share * span
    s = lax.axis_index("seq")
    g = lax.axis_index("chan")
    half = lax.div(s, half_count)
    place = lax.rem(s, half_count)

    ring = half_count // 2
    near = [(turn, core) for turn in range(ring) for core in (0, 1)]
    near.sort(key=lambda at: -min(at[0], ring - at[0]))

    def place_at(turn, core):
        return jnp.bitwise_xor(jnp.bitwise_and(place + 2 * turn, half_count - 1), core)

    half_peers = [place_at(turn, core) for turn, core in near if turn or core]
    seq_peers = [(1 - half, place_at(turn, core)) for turn, core in near]
    seq_peers = seq_peers + [(half, peer) for peer in half_peers]
    chan_order = sorted(range(1, groups), key=lambda d: -(min(d // 4, 4 - d // 4) + d % 4))
    chan_peers = [jnp.bitwise_and(g + d, groups - 1) for d in chan_order]

    barrier = pltpu.get_barrier_semaphore()
    for other, peer in seq_peers:
        pl.semaphore_signal(
            barrier, inc=1, device_id={"seq": other * half_count + peer}, device_id_type=MESH
        )
    for peer in chan_peers:
        pl.semaphore_signal(barrier, inc=1, device_id={"chan": peer}, device_id_type=MESH)

    def remote(src, dst, index, device):
        pltpu.make_async_remote_copy(
            src_ref=src,
            dst_ref=dst,
            send_sem=send_sem.at[index],
            recv_sem=recv_sem.at[index],
            device_id=device,
            device_id_type=MESH,
        ).start()

    def to_seq(index, src_of, dst):
        for other, peer in seq_peers:
            remote(src_of(other, peer), dst, index, {"seq": other * half_count + peer})
        pltpu.make_async_copy(src_of(half, place), dst, recv_sem.at[index]).start()

    def to_half(index, src_of, dst):
        for peer in half_peers:
            remote(src_of(peer), dst, index, {"seq": half * half_count + peer})
        pltpu.make_async_copy(src_of(place), dst, recv_sem.at[index]).start()

    def to_chan(index, src_of, dst):
        for peer in chan_peers:
            remote(src_of(peer), dst, index, {"chan": peer})
        pltpu.make_async_copy(src_of(g), dst, recv_sem.at[index]).start()

    def arrived(index, ref):
        pltpu.make_async_copy(ref, ref, recv_sem.at[index]).wait()

    def sent(index, ref):
        pltpu.make_async_copy(ref, ref, send_sem.at[index]).wait()

    for fetch in fetches[:4]:
        fetch.wait()
    values_t = values[...].astype(F32)
    inner_t = gate_inner[...].astype(F32)
    high_one, low_one = split(filter_one[...])
    high_two, low_two = split(filter_two[...])
    filter_rows = jnp.concatenate(
        [high_one.astype(F32), low_one.astype(F32), high_two.astype(F32), low_two.astype(F32)], axis=0
    )
    for p in range(half_count):
        stage[p, 0:share, :] = values_t[p * share : (p + 1) * share]
        stage[p, share : 2 * share, :] = inner_t[p * share : (p + 1) * share]
        stage[p, 2 * share : 2 * share + 4, :] = filter_rows
        if 2 * share + 4 < row1:
            stage[p, 2 * share + 4 : row1, :] = jnp.zeros((row1 - 2 * share - 4, LANES), F32)
    send1[...] = stage[...].astype(BF16)
    pl.semaphore_wait(barrier, blocks + groups - 2)
    to_seq(0, lambda other, peer: send1.at[peer], recv1.at[s])

    for fetch in fetches[4:]:
        fetch.wait()
    outer_t[...] = gate_outer[...].astype(F32)
    teach_t[...] = teacher[...].astype(F32)
    vocab = gene_weights.shape[0]
    whole = vocab // LANES
    table[whole - whole % 8 :, :] = jnp.zeros((table.shape[0] - whole + whole % 8, LANES), F32)
    for line in range(whole):
        table[line : line + 1, :] = gene_weights[pl.ds(line * LANES, LANES)].reshape(1, LANES)
    if vocab % LANES:
        rest = gene_weights[pl.ds(whole * LANES, vocab % LANES)].reshape(1, vocab % LANES)
        table[whole : whole + 1, 0 : vocab % LANES] = rest
    ids = gene_ids[...]
    hot_rows = (
        lax.broadcasted_iota(jnp.int32, (table.shape[0], LANES), 0) == lax.shift_right_logical(ids, 7)
    ).astype(F32)
    picked = tn(table[...], hot_rows, HIGHEST)
    hot_lanes = lax.broadcasted_iota(jnp.int32, (LANES, LANES), 0) == jnp.bitwise_and(ids, 127)
    weight = jnp.sum(jnp.where(hot_lanes, picked, 0.0), axis=0, keepdims=True)
    token = s * LANES + lax.broadcasted_iota(jnp.int32, (1, LANES), 1)
    opening = token == 0
    start = cell_lengths[0]
    for cell in range(1, cell_lengths.shape[0]):
        opening = jnp.logical_or(opening, token == start)
        start = start + cell_lengths[cell]
    token_w[...] = jnp.where(opening, 0.0, weight)
    edge = pad.shape[0] - rows
    edge = edge // 2
    for first in (0, edge + rows):
        pad[first : first + edge, :] = jnp.zeros((edge, LANES), F32)
    empty = jnp.zeros((rows, span * LANES), BF16)
    wide_one[0:rows, :] = empty
    wide_two[0:rows, :] = empty
    wide_back[rows : 2 * rows, :] = empty

    row_iota = lax.broadcasted_iota(jnp.int32, (LANES, LANES), 0)
    lane_iota = lax.broadcasted_iota(jnp.int32, (LANES, LANES), 1)
    flip = (row_iota + lane_iota == LANES - 1).astype(BF16)
    row8 = lax.broadcasted_iota(jnp.int32, (8, LANES), 0)
    lane8 = lax.broadcasted_iota(jnp.int32, (8, LANES), 1)
    tiles = LANES // 8

    def staggered(block, first):
        return pltpu.roll(block, first, axis=1, stride=1, stride_axis=0)

    def turn(block, amount):
        return pltpu.roll(block, amount, axis=1) if amount else block

    def toeplitz_block(row, before, write, upper):
        base = staggered(jnp.broadcast_to(row, (8, LANES)), 1 if upper else 0)
        turned = [turn(base, 8 * j) for j in range(tiles)]
        for j in range(0, tiles, 2):
            pair = []
            for i in (j, j + 1):
                keep = lane8 <= row8 + 8 * i if upper else lane8 >= row8 + 8 * i
                pair.append(jnp.where(keep, turned[i], before[i]))
            high, low = split(jnp.concatenate(pair, axis=0))
            write(8 * j, high, low)
        return turned

    def toeplitz_loop(lags, toe):
        def body(m, before):
            def write(first, high, low):
                at = pl.ds(pl.multiple_of(m * LANES + first, 16), 16)
                toe[at, 0:LANES] = high
                toe[at, LANES : 2 * LANES] = low

            return tuple(toeplitz_block(lags[pl.ds(m, 1), :], before, write, True))

        lax.fori_loop(0, blocks, body, (jnp.zeros((8, LANES), F32),) * tiles)

    def toeplitz_step(lags, toe, step, before):
        for m in range(step * span, (step + 1) * span):

            def write(first, high, low):
                at = slice(m * LANES + first, m * LANES + first + 16)
                toe[at, 0:LANES] = high
                toe[at, LANES : 2 * LANES] = low

            before = toeplitz_block(lags[m : m + 1, :], before, write, False)
        return before

    def weights_of(toe, step):
        return toe[step * span * LANES : (step + 1) * span * LANES, :]

    def joined(product):
        return product[:, 0:LANES] + product[:, LANES : 2 * LANES]

    def widen(wide, first, direction):
        for j in range(span):
            at = edge + direction * share * j
            wide[first : first + rows, j * LANES : (j + 1) * LANES] = pad[at : at + rows, :].astype(BF16)

    own_at = pl.ds(multiple(half, own_rows), own_rows)
    arrived(0, recv1)
    to_chan(
        1,
        lambda peer: w_out.at[:, pl.ds(multiple(lax.div(peer, 2), LANES), LANES)],
        w_blocks.at[g],
    )
    flat1[...] = recv1[...].astype(F32).reshape(blocks * row1, LANES)

    def every(first):
        return flat1[pl.ds(first, blocks, stride=row1), :]

    lags_one[...] = every(2 * share) + every(2 * share + 1)
    lags_two[...] = every(2 * share + 2) + every(2 * share + 3)
    for c in range(share):
        pad[pl.ds(edge + c, blocks, stride=share), :] = every(c)
        gate_c[pl.ds(c, blocks, stride=share), :] = every(share + c)
    widen(wide_one, rows, -1)
    before = [jnp.zeros((8, LANES), F32)] * tiles
    for step in range(steps):
        before = toeplitz_step(lags_one, toe_one, step, before)
        part = nn(wide_one[rows : 2 * rows - shift * step, :], weights_of(toe_one, step))
        if step == 0:
            total[...] = part
        else:
            total[shift * step : rows, :] += part
    first_conv = joined(total[...])
    conv_c[...] = first_conv
    pad[edge : edge + rows, :] = gate_c[...] * first_conv
    widen(wide_two, rows, -1)
    before = [jnp.zeros((8, LANES), F32)] * tiles
    product = jnp.zeros((own_rows, 2 * LANES), F32)
    for step in range(steps):
        before = toeplitz_step(lags_two, toe_two, step, before)
        at = pl.multiple_of(rows + half * own_rows - shift * step, shift)
        product = product + nn(wide_two[pl.ds(at, own_rows), :], weights_of(toe_two, step))
    send2[...] = joined(product).reshape(half_count, share, LANES)
    to_half(2, lambda peer: send2.at[peer], recv2.at[place])

    back_two[...] = nn(every(2 * share + 2).astype(BF16), flip) + nn(every(2 * share + 3).astype(BF16), flip)
    toeplitz_loop(back_two, upper_two)
    arrived(1, w_blocks)
    stacked = w_blocks[...].astype(F32).reshape(groups * channels, LANES)
    w_rows[...] = stacked.T.astype(BF16)

    arrived(2, recv2)
    second_t[...] = recv2[...].reshape(channels, LANES)
    pooled_t[...] = (outer_t[...] * second_t[...]).astype(BF16)
    to_chan(3, lambda peer: pooled_t, pooled_all.at[g])
    back_one[...] = nn(every(2 * share).astype(BF16), flip) + nn(every(2 * share + 1).astype(BF16), flip)
    toeplitz_loop(back_one, upper_one)
    arrived(3, pooled_all)
    width = groups * channels
    pooled = pooled_all[...].reshape(width, LANES)
    output = nn(w_out[...], pooled)
    deviation = (token_w[...] * (output - teach_t[...])).astype(BF16)
    dev_t[...] = deviation
    to_chan(4, lambda peer: dev_t, dev_all.at[g])

    share_w = width // blocks
    half_w = share_w // 2
    parts = pooled.reshape(blocks, 2, half_w, LANES)
    left = jnp.concatenate(
        [parts[:, 0].reshape(blocks * half_w, LANES), parts[:, 1].reshape(blocks * half_w, LANES)], axis=1
    )
    blank = jnp.zeros_like(deviation)
    right = jnp.concatenate(
        [jnp.concatenate([deviation, blank], axis=1), jnp.concatenate([blank, deviation], axis=1)], axis=0
    )
    gw_send[...] = nt(left, right).reshape(blocks, half_w, LANES).astype(gw_send.dtype)

    arrived(4, dev_all)
    back_outer = nn(
        w_rows[pl.ds(multiple(lax.rem(g, 2), channels), channels), :], dev_all[...].reshape(width, LANES)
    )
    back_second = back_outer * outer_t[...]
    send5[...] = back_second.astype(BF16).reshape(half_count, share, LANES)
    to_seq(6, lambda other, peer: send5.at[peer], recv5.at[s])
    to_seq(5, lambda other, peer: gw_send.at[other * half_count + peer], gw_recv.at[s])
    out_outer[...] = (back_outer * second_t[...]).astype(BF16)

    arrived(6, recv5)
    signal = recv5[...].astype(F32).reshape(rows, LANES)
    pad[edge : edge + rows, :] = signal
    widen(wide_back, 0, 1)
    for step in range(steps):
        part = nn(wide_back[shift * step : rows, :], weights_of(upper_two, step))
        if step == 0:
            total[...] = part
        else:
            total[0 : rows - shift * step, :] += part
    back_inner = joined(total[...])
    back_first = back_inner * gate_c[...]
    pad[edge : edge + rows, :] = back_first
    conv_c[...] = back_inner * conv_c[...]
    widen(wide_back, 0, 1)
    product = jnp.zeros((own_rows, 2 * LANES), F32)
    for step in range(steps):
        at = pl.multiple_of(half * own_rows + shift * step, shift)
        product = product + nn(wide_back[pl.ds(at, own_rows), :], weights_of(upper_one, step))
    grad_values_c = joined(product)
    grad_inner_c = conv_c[own_at, :]
    for p in range(half_count):
        at = slice(p * share, (p + 1) * share)
        flat6[p * row6 : p * row6 + share, :] = grad_values_c[at]
        flat6[p * row6 + share : p * row6 + 2 * share, :] = grad_inner_c[at]

    def filter_grad(back, wide, column):
        turned = nt(flip, back.astype(BF16)).astype(BF16)
        for j in range(half_count // span):
            at = pl.multiple_of(rows - half * own_rows - shift * j, shift)
            cross[:, j * span * LANES : (j + 1) * span * LANES] = nn(turned, wide[pl.ds(at, rows), :])
        at = multiple(1 - half, own_rows)
        cross[:, half_count * LANES : (half_count + 1) * LANES] = nn(turned, wide[pl.ds(at, rows), 0:LANES])

        def block(m):
            return [
                turn(cross[8 * j : 8 * j + 8, m * LANES : (m + 1) * LANES], 8 * j) for j in range(tiles)
            ]

        def added(terms):
            while len(terms) > 1:
                terms = [a + b for a, b in zip(terms[::2], terms[1::2])]
            return terms[0]

        later = block(half_count)
        later = staggered(added([jnp.where(lane8 >= 8 * j, later[j], 0.0) for j in range(tiles)]), 0), later
        for m in range(half_count - 1, -1, -1):
            after_sum, after = later
            current = block(m)
            here = staggered(
                added([jnp.where(lane8 >= 8 * j, current[j], after[j]) for j in range(tiles)]), 0
            )
            sums[m : m + 1, :] = jnp.sum(jnp.where(lane8 >= row8, here, after_sum), axis=0, keepdims=True)
            later = here, current
        high, low = split(sums[...])
        flat6[pl.ds(column, half_count, stride=row6), :] = high.astype(F32)
        flat6[pl.ds(column + 1, half_count, stride=row6), :] = low.astype(F32)

    filter_grad(signal, wide_two, 2 * share + 2)
    filter_grad(back_first, wide_one, 2 * share)
    for c in range(2 * share + 4, row6):
        flat6[pl.ds(c, half_count, stride=row6), :] = jnp.zeros((half_count, LANES), F32)
    send6[...] = flat6[...].reshape(half_count, row6, LANES).astype(BF16)
    to_half(7, lambda peer: send6.at[peer], recv6.at[place])

    arrived(5, gw_recv)
    total_w = jnp.sum(gw_recv[...].astype(F32), axis=0)
    out_w[0:half_w, :] = total_w[:, 0:channels]
    out_w[half_w:share_w, :] = total_w[:, channels : 2 * channels]

    sent(0, recv1.at[pl.ds(0, blocks - 1)])
    sent(1, w_blocks.at[pl.ds(0, groups - 1)])
    sent(2, recv2.at[pl.ds(0, half_count - 1)])
    sent(3, pooled_all.at[pl.ds(0, groups - 1)])
    sent(4, dev_all.at[pl.ds(0, groups - 1)])
    sent(5, gw_recv.at[pl.ds(0, blocks - 1)])
    sent(6, recv5.at[pl.ds(0, blocks - 1)])
    arrived(7, recv6)
    flat6[...] = recv6[...].astype(F32).reshape(half_count * row6, LANES)
    for p in range(half_count):
        at = slice(p * share, (p + 1) * share)
        second_t[at, :] = flat6[p * row6 : p * row6 + share, :]
        outer_t[at, :] = flat6[p * row6 + share : p * row6 + 2 * share, :]
    out_values[...] = second_t[...].astype(BF16)
    out_inner[...] = outer_t[...].astype(BF16)
    lag_rows = []
    for column in (2 * share, 2 * share + 2):
        both = flat6[pl.ds(column, half_count, stride=row6), :] + flat6[
            pl.ds(column + 1, half_count, stride=row6), :
        ]
        lag_rows.append(jnp.sum(both, axis=0, keepdims=True))
    lag_rows.append(jnp.zeros((6, LANES), F32))
    ordered = nn(jnp.concatenate(lag_rows, axis=0), flip.astype(F32), HIGHEST)
    out_one[...] = ordered[0:1]
    out_two[...] = ordered[1:2]
    sent(7, recv6.at[pl.ds(0, half_count - 1)])


def hand_on(*refs):
    count = len(refs) // 2
    for source, target in zip(refs[:count], refs[count:]):
        target[...] = source[...]


def rounded(count, factor):
    return -(-count // factor) * factor


def per_device(
    blocks,
    groups,
    values,
    gate_inner,
    gate_outer,
    filter_one,
    filter_two,
    teacher,
    w_out,
    gene_ids,
    cell_lengths,
    gene_weights,
):
    length, channels = values.shape
    half_count = blocks // 2
    share = channels // half_count
    rows = share * blocks
    width = groups * channels
    share_w = width // blocks
    row1 = rounded(2 * share + 4, 16)
    span = max(1, 16 // share)
    vocab = gene_weights.shape[0]
    vmem = pl.BlockSpec(memory_space=pltpu.VMEM)
    V = pltpu.VMEM
    grads = pl.pallas_call(
        functools.partial(kernel, blocks, groups),
        out_shape=(
            jax.ShapeDtypeStruct((channels, length), BF16),
            jax.ShapeDtypeStruct((channels, length), BF16),
            jax.ShapeDtypeStruct((channels, length), BF16),
            jax.ShapeDtypeStruct((1, LANES), F32),
            jax.ShapeDtypeStruct((1, LANES), F32),
            jax.ShapeDtypeStruct((share_w, channels), F32),
        ),
        in_specs=[pl.BlockSpec(memory_space=pltpu.HBM)] * 10,
        out_specs=(vmem,) * 6,
        scratch_shapes=[
            V((channels, length), BF16),
            V((channels, length), BF16),
            V((channels, length), BF16),
            V((channels, length), BF16),
            V((1, LANES), F32),
            V((1, LANES), F32),
            V((channels, width), BF16),
            V((1, LANES), jnp.int32),
            pltpu.SMEM(cell_lengths.shape, jnp.int32),
            V((vocab,), F32),
            V((half_count, row1, LANES), F32),
            V((half_count, row1, LANES), BF16),
            V((blocks, row1, LANES), BF16),
            V((blocks * row1, LANES), F32),
            V((rows + 32, LANES), F32),
            V((rows, LANES), F32),
            V((rows, LANES), F32),
            V((blocks, LANES), F32),
            V((blocks, LANES), F32),
            V((blocks, LANES), F32),
            V((blocks, LANES), F32),
            V((2 * rows, span * LANES), BF16),
            V((2 * rows, span * LANES), BF16),
            V((2 * rows, span * LANES), BF16),
            V((blocks * LANES, 2 * LANES), BF16),
            V((blocks * LANES, 2 * LANES), BF16),
            V((blocks * LANES, 2 * LANES), BF16),
            V((blocks * LANES, 2 * LANES), BF16),
            V((rows, 2 * LANES), F32),
            V((half_count, share, LANES), F32),
            V((half_count, share, LANES), F32),
            V((channels, LANES), F32),
            V((channels, LANES), F32),
            V((channels, LANES), F32),
            V((groups, channels, LANES), BF16),
            V((LANES, width), BF16),
            V((1, LANES), F32),
            V((rounded(vocab, 8 * LANES) // LANES, LANES), F32),
            V((channels, LANES), BF16),
            V((groups, channels, LANES), BF16),
            V((channels, LANES), BF16),
            V((groups, channels, LANES), BF16),
            V((blocks, share_w // 2, LANES), BF16),
            V((blocks, share_w // 2, LANES), BF16),
            V((half_count, share, LANES), BF16),
            V((blocks, share, LANES), BF16),
            V((LANES, (half_count + 1) * LANES), F32),
            V((half_count, LANES), F32),
            V((half_count * row1, LANES), F32),
            V((half_count, row1, LANES), BF16),
            V((half_count, row1, LANES), BF16),
            pltpu.SemaphoreType.DMA((8,)),
            pltpu.SemaphoreType.DMA((8,)),
            pltpu.SemaphoreType.DMA((10,)),
        ],
        compiler_params=pltpu.CompilerParams(
            collective_id=0, has_side_effects=True, vmem_limit_bytes=48 << 20
        ),
    )(
        *(
            pltpu.with_memory_space_constraint(operand, pltpu.HBM)
            for operand in (
                values.T,
                gate_inner.T,
                gate_outer.T,
                teacher.T,
                filter_one,
                filter_two,
                w_out.T,
                gene_ids.reshape(1, LANES),
                cell_lengths,
                gene_weights,
            )
        )
    )
    grads = pl.pallas_call(
        hand_on,
        out_shape=tuple(jax.ShapeDtypeStruct(grad.shape, grad.dtype) for grad in grads),
        in_specs=[vmem] * 6,
        out_specs=(vmem,) * 6,
        compiler_params=pltpu.CompilerParams(vmem_limit_bytes=1 << 20),
    )(*grads)
    return (grads[0].T, grads[1].T, grads[2].T) + tuple(grads[3:])


def solution(mesh):
    blocks, groups = mesh.shape["seq"], mesh.shape["chan"]
    return jax.shard_map(
        functools.partial(per_device, blocks, groups),
        mesh=mesh,
        in_specs=(
            P("seq", "chan"),
            P("seq", "chan"),
            P("seq", "chan"),
            P("chan", "seq"),
            P("chan", "seq"),
            P("seq", "chan"),
            P(None, "chan"),
            P("seq"),
            P(),
            P(),
        ),
        out_specs=(
            P("seq", "chan"),
            P("seq", "chan"),
            P("seq", "chan"),
            P("chan", "seq"),
            P("chan", "seq"),
            P("seq", "chan"),
        ),
        check_vma=False,
    )
```
